256 devices in a mesh: row: 16 (over z, core), col: 16 (over x, y).
Axes of the slice: x: 4, y: 4, z: 8, core: 2. Of those that a mesh axis runs over, the one named last changes fastest.
Arguments:
- tokens: bfloat16 [4096, 8192], P('row', 'col'), may hold values from -6 to 6
- out_grad: bfloat16 [4096, 8192], P('row', 'col'), may hold values from -1.5 to 1.5
- gate_weight: bfloat16 [112, 1024, 128], P('col', 'row'), may hold values from -0.1875 to 0.1875
- up_weight: bfloat16 [112, 1024, 128], P('col', 'row'), may hold values from -0.1875 to 0.1875
- down_weight: bfloat16 [112, 1024, 128], P('col', 'row'), may hold values from -0.125 to 0.125
- gate_rows: int32 [112, 8], P('col'), may hold values from 0 to 63, all different within a row
- up_rows: int32 [112, 8], P('col'), may hold values from 0 to 63, all different within a row
- down_columns: int32 [112, 8], P('col'), may hold values from 0 to 63, all different within a row
Outputs:
- output: bfloat16 [4096, 8192], P('row', 'col')
- input_grad: bfloat16 [4096, 8192], P('row', 'col')
- gate_weight_grad: bfloat16 [112, 1024, 128], P('col', 'row')
- up_weight_grad: bfloat16 [112, 1024, 128], P('col', 'row')
- down_weight_grad: bfloat16 [112, 1024, 128], P('col', 'row')
The draws below stay inside these ranges and needn't reach their ends.
Inputs may be any that keep to these rules, and one draw needn't show every extreme that they name: `gate_rows`: each row names 8 different block-rows; every block-row is named in some row. `up_rows`: each row names 8 different block-rows; every block-row is named in some row. `down_columns`: each row names 8 different output block-columns; every block-column is named in some row.
All inputs are finite; a program needn't handle non-finite values.
Results may differ from the reference program's by a relative error of at most 0.018.
Values may be sent and summed in bfloat16 or wider, within the bound.
A program may use at most 128 MiB of HBM per device.

```python
import jax
import jax.numpy as jnp
from jax import lax

D = 8192
BS = 128
KG = 8
KH = 8
TOK_ROW = 256
DB = 64
FB = 112
FBC = 7
TOKENS = 4096
N_ROW = 16
N_COL = 16


def shard_levels(key, extent, shards, low, high):
    factor_of = 1.0
    for dim, shards_of in shards:
        steps = jax.random.uniform(jax.random.fold_in(jax.random.fold_in(key, 6), dim), (shards_of,), jnp.float32, low / len(shards), high / len(shards))
        factor_of = factor_of * jnp.repeat(jnp.exp(steps), extent[dim] // shards_of).reshape((-1,) + (1,) * (len(extent) - 1 - dim))
    return factor_of


def distinct(key, rows, number_of, top, lift):
    ranking = jax.random.permutation(jax.random.fold_in(key, 1), number_of)
    boost = ranking
    for power in range(3):
        boost = boost * boost // number_of
    boost = boost * lift // number_of
    chance = jax.random.randint(jax.random.fold_in(key, 2), (rows, number_of), 0, 4096) + boost
    fixed_rows = jax.random.permutation(jax.random.fold_in(key, 3), rows)[jnp.arange(number_of) % rows]
    chance = jnp.where(jnp.arange(rows)[:, None] == fixed_rows[None, :], 1 << 14, chance)
    score = chance * number_of + jnp.arange(number_of)
    return lax.top_k(score.astype(jnp.int32), top)[1].astype(jnp.int32)


def noise(stream_key, shape, deviation, limit, pieces=(), held_as=jnp.bfloat16):
    loudness = shard_levels(stream_key, shape, pieces, -0.22, 0.18) if pieces else 1.0
    array = jax.random.normal(stream_key, shape, jnp.float32) * deviation * loudness
    return jnp.minimum(jnp.maximum(array, -limit), limit).astype(held_as)


def setup_inputs(seed: int = 0) -> dict:
    keys = jax.random.split(jax.random.key(seed), 9)
    return {
        "tokens": noise(keys[0], (TOKENS, D), 1.0, 6.0, ((0, 16), (1, 16))),
        "out_grad": noise(keys[1], (TOKENS, D), 0.25, 1.5, ((0, 16), (1, 16))),
        "gate_weight": noise(keys[2], (FB, KG * BS, BS), (KG * BS) ** -0.5, 0.1875, ((0, 16), (1, 16))),
        "up_weight": noise(keys[3], (FB, KG * BS, BS), (KG * BS) ** -0.5, 0.1875, ((0, 16), (1, 16))),
        "down_weight": noise(keys[4], (FB, KH * BS, BS), (FB * KH * BS // DB) ** -0.5, 0.125, ((0, 16), (1, 16))),
        "gate_rows": distinct(keys[5], FB, DB, KG, 0),
        "up_rows": distinct(keys[6], FB, DB, KG, 1024),
        "down_columns": distinct(keys[7], FB, DB, KH, 2048),
    }


def rounded(values):
    return lax.optimization_barrier(values.astype(jnp.bfloat16)).astype(jnp.float32)


def spread(contrib, block_lists):
    zero_block = jnp.zeros((TOKENS, DB, BS), jnp.float32)
    return zero_block.at[:, block_lists.reshape(-1)].add(contrib.reshape(TOKENS, -1, BS))


def by_group(values):
    return values.reshape((N_ROW, TOK_ROW) + values.shape[1:])


def group_sum(partial_value):
    return jnp.sum(rounded(partial_value), axis=0).astype(jnp.bfloat16)


def reference(tokens, out_grad, gate_weight, up_weight, down_weight, gate_rows, up_rows, down_columns):
    highest = lax.Precision.HIGHEST
    blocks_in = tokens.astype(jnp.float32).reshape(TOKENS, DB, BS)
    blocks_grad = out_grad.astype(jnp.float32).reshape(TOKENS, DB, BS)

    def column(totals, column_index):
        out_total, in_total = totals
        first_slot = column_index * FBC
        gate_tiles = lax.dynamic_slice_in_dim(gate_weight, first_slot, FBC, 0).astype(jnp.float32).reshape(FBC, KG, BS, BS)
        up_tiles = lax.dynamic_slice_in_dim(up_weight, first_slot, FBC, 0).astype(jnp.float32).reshape(FBC, KG, BS, BS)
        down_tiles = lax.dynamic_slice_in_dim(down_weight, first_slot, FBC, 0).astype(jnp.float32).reshape(FBC, KH, BS, BS)
        gate_list = lax.dynamic_slice_in_dim(gate_rows, first_slot, FBC, 0)
        up_list = lax.dynamic_slice_in_dim(up_rows, first_slot, FBC, 0)
        down_list = lax.dynamic_slice_in_dim(down_columns, first_slot, FBC, 0)
        picked_gate = jnp.take(blocks_in, gate_list.reshape(-1), axis=1).reshape(TOKENS, FBC, KG, BS)
        picked_up = jnp.take(blocks_in, up_list.reshape(-1), axis=1).reshape(TOKENS, FBC, KG, BS)
        picked_grad = jnp.take(blocks_grad, down_list.reshape(-1), axis=1).reshape(TOKENS, FBC, KH, BS)
        gate_value = jnp.einsum('tfkr,fkri->tfi', picked_gate, gate_tiles, precision=highest)
        up_value = jnp.einsum('tfkr,fkri->tfi', picked_up, up_tiles, precision=highest)
        sigmoid_gate = jax.nn.sigmoid(gate_value)
        silu_gate = gate_value * sigmoid_gate
        hidden = rounded(silu_gate * up_value)
        out_part = jnp.einsum('tfi,fkji->tfkj', hidden, down_tiles, precision=highest)
        out_total = out_total + rounded(spread(out_part, down_list))
        hidden_grad = jnp.einsum('tfkj,fkji->tfi', picked_grad, down_tiles, precision=highest)
        gate_grad = rounded(hidden_grad * up_value * sigmoid_gate * (1.0 + gate_value * (1.0 - sigmoid_gate)))
        up_grad = rounded(hidden_grad * silu_gate)
        from_gate = jnp.einsum('tfi,fkri->tfkr', gate_grad, gate_tiles, precision=highest)
        from_up = jnp.einsum('tfi,fkri->tfkr', up_grad, up_tiles, precision=highest)
        in_total = in_total + rounded(spread(from_gate, gate_list) + spread(from_up, up_list))
        gate_tile_grad = group_sum(jnp.einsum('ntfkr,ntfi->nfkri', by_group(picked_gate), by_group(gate_grad), precision=highest))
        up_tile_grad = group_sum(jnp.einsum('ntfkr,ntfi->nfkri', by_group(picked_up), by_group(up_grad), precision=highest))
        down_tile_grad = group_sum(jnp.einsum('ntfkj,ntfi->nfkji', by_group(picked_grad), by_group(hidden), precision=highest))
        return (out_total, in_total), (gate_tile_grad, up_tile_grad, down_tile_grad)

    initial = (jnp.zeros((TOKENS, DB, BS), jnp.float32), jnp.zeros((TOKENS, DB, BS), jnp.float32))
    totals, tile_grads = lax.scan(column, initial, jnp.arange(N_COL, dtype=jnp.int32))
    output = totals[0].reshape(TOKENS, D).astype(jnp.bfloat16)
    input_grad = totals[1].reshape(TOKENS, D).astype(jnp.bfloat16)
    return (output, input_grad, tile_grads[0].reshape(FB, KG * BS, BS), tile_grads[1].reshape(FB, KG * BS, BS), tile_grads[2].reshape(FB, KH * BS, BS))
```

```python
import jax
import jax.numpy as jnp
from jax import lax
from jax.sharding import PartitionSpec as P

D = 8192
BS = 128
KG = 8
KH = 8
DB = 64


def spread(contrib, block_lists):
    rows_here = contrib.shape[0]
    zero_block = jnp.zeros((rows_here, DB, BS), jnp.float32)
    placed = zero_block.at[:, block_lists.reshape(-1)].add(contrib.reshape(rows_here, -1, BS))
    return placed.reshape(rows_here, D)


def shards(tokens, out_grad, gate_weight, up_weight, down_weight, gate_rows, up_rows, down_columns):
    panels = lax.all_gather(jnp.stack([tokens, out_grad]), "col", axis=2, tiled=True)
    panel_in, panel_grad = panels[0], panels[1]
    rows_here = panel_in.shape[0]
    owned_slots = gate_weight.shape[0]
    tiles = lax.all_gather(
        jnp.concatenate([gate_weight, up_weight, down_weight], axis=0), "row", axis=1, tiled=True
    )
    gate_tiles = tiles[:owned_slots]
    up_tiles = tiles[owned_slots : 2 * owned_slots]
    down_tiles = tiles[2 * owned_slots :]
    gate_four = gate_tiles.reshape(owned_slots, KG, BS, BS)
    up_four = up_tiles.reshape(owned_slots, KG, BS, BS)
    blocks_in = panel_in.reshape(rows_here, DB, BS)
    picked_gate = jnp.take(blocks_in, gate_rows.reshape(-1), axis=1).reshape(
        rows_here, owned_slots, KG, BS
    )
    picked_up = jnp.take(blocks_in, up_rows.reshape(-1), axis=1).reshape(
        rows_here, owned_slots, KG, BS
    )
    gate_value = jnp.einsum(
        "tfkr,fkri->tfi", picked_gate, gate_four, preferred_element_type=jnp.float32
    )
    up_value = jnp.einsum("tfkr,fkri->tfi", picked_up, up_four, preferred_element_type=jnp.float32)
    sigmoid_gate = jax.nn.sigmoid(gate_value)
    silu_gate = gate_value * sigmoid_gate
    hidden = (silu_gate * up_value).astype(jnp.bfloat16)
    down_four = down_tiles.reshape(owned_slots, KH, BS, BS)
    out_part = jnp.einsum("tfi,fkji->tfkj", hidden, down_four, preferred_element_type=jnp.float32)
    partial_out = spread(out_part, down_columns)
    blocks_grad = panel_grad.reshape(rows_here, DB, BS)
    picked_grad = jnp.take(blocks_grad, down_columns.reshape(-1), axis=1).reshape(
        rows_here, owned_slots, KH, BS
    )
    hidden_grad = jnp.einsum(
        "tfkj,fkji->tfi", picked_grad, down_four, preferred_element_type=jnp.float32
    )
    gate_grad = (
        hidden_grad * up_value * sigmoid_gate * (1.0 + gate_value * (1.0 - sigmoid_gate))
    ).astype(jnp.bfloat16)
    up_grad = (hidden_grad * silu_gate).astype(jnp.bfloat16)
    from_gate = jnp.einsum(
        "tfi,fkri->tfkr", gate_grad, gate_four, preferred_element_type=jnp.float32
    )
    from_up = jnp.einsum("tfi,fkri->tfkr", up_grad, up_four, preferred_element_type=jnp.float32)
    partial_in = spread(from_gate, gate_rows) + spread(from_up, up_rows)
    gate_partial = jnp.einsum(
        "tfkr,tfi->fkri", picked_gate, gate_grad, preferred_element_type=jnp.float32
    ).reshape(owned_slots, KG * BS, BS)
    up_partial = jnp.einsum(
        "tfkr,tfi->fkri", picked_up, up_grad, preferred_element_type=jnp.float32
    ).reshape(owned_slots, KG * BS, BS)
    down_partial = jnp.einsum(
        "tfkj,tfi->fkji", picked_grad, hidden, preferred_element_type=jnp.float32
    ).reshape(owned_slots, KH * BS, BS)
    tile_sums = lax.psum_scatter(
        jnp.concatenate([gate_partial, up_partial, down_partial], axis=0).astype(jnp.bfloat16),
        "row",
        scatter_dimension=1,
        tiled=True,
    )
    panel_sums = lax.psum_scatter(
        jnp.stack([partial_out, partial_in]).astype(jnp.bfloat16),
        "col",
        scatter_dimension=2,
        tiled=True,
    )
    return (
        panel_sums[0],
        panel_sums[1],
        tile_sums[:owned_slots],
        tile_sums[owned_slots : 2 * owned_slots],
        tile_sums[2 * owned_slots :],
    )


def solution(mesh):
    in_specs = (
        P("row", "col"),
        P("row", "col"),
        P("col", "row", None),
        P("col", "row", None),
        P("col", "row", None),
        P("col", None),
        P("col", None),
        P("col", None),
    )
    out_specs = (
        P("row", "col"),
        P("row", "col"),
        P("col", "row", None),
        P("col", "row", None),
        P("col", "row", None),
    )
    return jax.shard_map(shards, mesh=mesh, in_specs=in_specs, out_specs=out_specs, check_vma=False)
```

```python
import functools

import jax
import jax.numpy as jnp
from jax import lax
from jax.experimental import pallas as pl
from jax.experimental.pallas import tpu as pltpu
from jax.sharding import PartitionSpec as P

BS = 128
KG = 8
KH = 8


def core_kernel(slots, gr_ref, ur_ref, dc_ref, p_ref, w_ref, panel_ref, tiles_ref, out_acc, in_acc):
    out_acc[...] = jnp.zeros_like(out_acc)
    in_acc[...] = jnp.zeros_like(in_acc)
    f32 = jnp.float32
    bf16 = jnp.bfloat16
    rows = p_ref.shape[1]
    tn = (((0,), (0,)), ((), ()))
    nt = (((1,), (1,)), ((), ()))

    def col(b):
        return pl.ds(pl.multiple_of(b * BS, BS), BS)

    def body(f, carry):
        gate = jnp.zeros((rows, BS), f32)
        up = jnp.zeros((rows, BS), f32)
        hg = jnp.zeros((rows, BS), f32)
        for k in range(KG):
            ks = pl.ds(k * BS, BS)
            gate += jnp.dot(p_ref[0, :, col(gr_ref[f, k])], w_ref[f, ks, :], preferred_element_type=f32)
            up += jnp.dot(p_ref[0, :, col(ur_ref[f, k])], w_ref[slots + f, ks, :], preferred_element_type=f32)
            hg += jnp.dot(p_ref[1, :, col(dc_ref[f, k])], w_ref[2 * slots + f, ks, :], preferred_element_type=f32)
        sg = 1.0 / (1.0 + jnp.exp(-gate))
        silu = gate * sg
        hidden = (silu * up).astype(bf16)
        gg = (hg * up * sg * (1.0 + gate * (1.0 - sg))).astype(bf16)
        ug = (hg * silu).astype(bf16)
        for k in range(KG):
            ks = pl.ds(k * BS, BS)
            gt = w_ref[f, ks, :]
            ut = w_ref[slots + f, ks, :]
            dt = w_ref[2 * slots + f, ks, :]
            cd = col(dc_ref[f, k])
            cg = col(gr_ref[f, k])
            cu = col(ur_ref[f, k])
            out_acc[:, cd] += lax.dot_general(hidden, dt, nt, preferred_element_type=f32)
            in_acc[:, cg] += lax.dot_general(gg, gt, nt, preferred_element_type=f32)
            in_acc[:, cu] += lax.dot_general(ug, ut, nt, preferred_element_type=f32)
            tiles_ref[f, ks, :] = lax.dot_general(
                p_ref[0, :, cg], gg, tn, preferred_element_type=f32
            ).astype(bf16)
            tiles_ref[slots + f, ks, :] = lax.dot_general(
                p_ref[0, :, cu], ug, tn, preferred_element_type=f32
            ).astype(bf16)
            tiles_ref[2 * slots + f, ks, :] = lax.dot_general(
                p_ref[1, :, cd], hidden, tn, preferred_element_type=f32
            ).astype(bf16)
        return carry

    lax.fori_loop(0, slots, body, 0)
    panel_ref[0] = out_acc[...].astype(bf16)
    panel_ref[1] = in_acc[...].astype(bf16)


def core(panels, tiles, gate_rows, up_rows, down_columns):
    slots = gate_rows.shape[0]
    rows, width = panels.shape[1], panels.shape[2]
    smem = pl.BlockSpec(memory_space=pltpu.SMEM)
    vmem = pl.BlockSpec(memory_space=pltpu.VMEM)
    flops = 2 * rows * BS * BS * slots * KG * 9
    nbytes = 2 * (2 * panels.size + 2 * tiles.size)
    return pl.pallas_call(
        functools.partial(core_kernel, slots),
        out_shape=(
            jax.ShapeDtypeStruct((2, rows, width), jnp.bfloat16),
            jax.ShapeDtypeStruct(tiles.shape, jnp.bfloat16),
        ),
        in_specs=[smem, smem, smem, vmem, vmem],
        out_specs=(vmem, vmem),
        scratch_shapes=[
            pltpu.VMEM((rows, width), jnp.float32),
            pltpu.VMEM((rows, width), jnp.float32),
        ],
        compiler_params=pltpu.CompilerParams(vmem_limit_bytes=62 * 1024 * 1024),
        cost_estimate=pl.CostEstimate(
            flops=flops, transcendentals=rows * BS * slots, bytes_accessed=nbytes
        ),
    )(gate_rows, up_rows, down_columns, panels, tiles)


def shards(tokens, out_grad, gate_weight, up_weight, down_weight, gate_rows, up_rows, down_columns):
    owned_slots = gate_weight.shape[0]
    panels = lax.all_gather(jnp.stack([tokens, out_grad]), "col", axis=2, tiled=True)
    tiles = lax.all_gather(
        jnp.concatenate([gate_weight, up_weight, down_weight], axis=0), "row", axis=1, tiled=True
    )
    panel_part, tile_part = core(panels, tiles, gate_rows, up_rows, down_columns)
    tile_sums = lax.psum_scatter(tile_part, "row", scatter_dimension=1, tiled=True)
    panel_sums = lax.psum_scatter(panel_part, "col", scatter_dimension=2, tiled=True)
    return (
        panel_sums[0],
        panel_sums[1],
        tile_sums[:owned_slots],
        tile_sums[owned_slots : 2 * owned_slots],
        tile_sums[2 * owned_slots :],
    )


def solution(mesh):
    in_specs = (
        P("row", "col"),
        P("row", "col"),
        P("col", "row", None),
        P("col", "row", None),
        P("col", "row", None),
        P("col", None),
        P("col", None),
        P("col", None),
    )
    out_specs = (
        P("row", "col"),
        P("row", "col"),
        P("col", "row", None),
        P("col", "row", None),
        P("col", "row", None),
    )
    return jax.shard_map(shards, mesh=mesh, in_specs=in_specs, out_specs=out_specs, check_vma=False)
```

```python
import functools

import jax
import jax.numpy as jnp
from jax import lax
from jax.experimental import pallas as pl
from jax.experimental.pallas import tpu as pltpu
from jax.sharding import PartitionSpec as P

BS = 128
KG = 8
KH = 8


MESH = pl.DeviceIdType.MESH


def gather_rows_kernel(n_row, w_ref, out_ref, lsem, psend, precv, rsend, rrecv, fsend, frecv):
    me = lax.axis_index("row")
    n_chip = n_row // 2
    z = me // 2
    c = me % 2
    step_dir = 1 - 2 * c
    partner = z * 2 + (1 - c)
    nxt = ((z + step_dir + n_chip) % n_chip) * 2 + c
    prv = ((z - step_dir + n_chip) % n_chip) * 2 + c
    half = w_ref.shape[1]
    tile = 2 * half

    barrier = pltpu.get_barrier_semaphore()
    for peer in (partner, nxt, prv):
        pl.semaphore_signal(barrier, inc=1, device_id={"row": peer}, device_id_type=MESH)
    pl.semaphore_wait(barrier, 3)

    def chip_tile(p):
        return out_ref.at[:, pl.ds(pl.multiple_of(p * tile, tile), tile), :]

    own = out_ref.at[:, pl.ds(pl.multiple_of(z * tile + c * half, half), half), :]
    local = pltpu.make_async_copy(w_ref, own, lsem)
    local.start()
    swap = pltpu.make_async_remote_copy(
        src_ref=w_ref, dst_ref=own, send_sem=psend, recv_sem=precv,
        device_id={"row": partner}, device_id_type=MESH,
    )
    swap.start()
    local.wait()
    theirs = out_ref.at[:, pl.ds(pl.multiple_of(z * tile + (1 - c) * half, half), half), :]
    pltpu.make_async_remote_copy(
        src_ref=w_ref, dst_ref=theirs, send_sem=psend, recv_sem=precv,
        device_id={"row": partner}, device_id_type=MESH,
    ).wait_recv()
    swap.wait_send()

    steps = n_chip // 2
    sends = []
    fwds = []
    for s in range(1, steps + 1):
        p_send = (z - (s - 1) * step_dir + n_chip * steps) % n_chip
        p_recv = (z - s * step_dir + n_chip * steps) % n_chip
        ring = pltpu.make_async_remote_copy(
            src_ref=chip_tile(p_send), dst_ref=chip_tile(p_send),
            send_sem=rsend.at[s - 1], recv_sem=rrecv.at[s - 1],
            device_id={"row": nxt}, device_id_type=MESH,
        )
        ring.start()
        sends.append(ring)
        pltpu.make_async_remote_copy(
            src_ref=chip_tile(p_recv), dst_ref=chip_tile(p_recv),
            send_sem=rsend.at[s - 1], recv_sem=rrecv.at[s - 1],
            device_id={"row": prv}, device_id_type=MESH,
        ).wait_recv()
        if s < steps:
            fwd = pltpu.make_async_remote_copy(
                src_ref=chip_tile(p_recv), dst_ref=chip_tile(p_recv),
                send_sem=fsend.at[s - 1], recv_sem=frecv.at[s - 1],
                device_id={"row": partner}, device_id_type=MESH,
            )
            fwd.start()
            fwds.append(fwd)
    for s in range(1, steps):
        p_in = (z + s * step_dir + n_chip * steps) % n_chip
        pltpu.make_async_remote_copy(
            src_ref=chip_tile(p_in), dst_ref=chip_tile(p_in),
            send_sem=fsend.at[s - 1], recv_sem=frecv.at[s - 1],
            device_id={"row": partner}, device_id_type=MESH,
        ).wait_recv()
    for cp in sends + fwds:
        cp.wait_send()


def gather_rows(w, n_row):
    slots, half, width = w.shape
    steps = n_row // 4
    any_spec = pl.BlockSpec(memory_space=pl.ANY)
    return pl.pallas_call(
        functools.partial(gather_rows_kernel, n_row),
        out_shape=jax.ShapeDtypeStruct((slots, half * n_row, width), w.dtype),
        in_specs=[any_spec],
        out_specs=any_spec,
        scratch_shapes=[
            pltpu.SemaphoreType.DMA(()),
            pltpu.SemaphoreType.DMA(()),
            pltpu.SemaphoreType.DMA(()),
            pltpu.SemaphoreType.DMA((steps,)),
            pltpu.SemaphoreType.DMA((steps,)),
            pltpu.SemaphoreType.DMA((steps - 1,)),
            pltpu.SemaphoreType.DMA((steps - 1,)),
        ],
        compiler_params=pltpu.CompilerParams(collective_id=0, has_side_effects=True),
        cost_estimate=pl.CostEstimate(flops=0, transcendentals=0, bytes_accessed=2 * w.size * n_row),
    )(w)


def core_kernel(slots, gr_ref, ur_ref, dc_ref, p_ref, w_ref, panel_ref, tiles_ref, out_acc, in_acc):
    out_acc[...] = jnp.zeros_like(out_acc)
    in_acc[...] = jnp.zeros_like(in_acc)
    f32 = jnp.float32
    bf16 = jnp.bfloat16
    rows = p_ref.shape[1]
    tn = (((0,), (0,)), ((), ()))
    nt = (((1,), (1,)), ((), ()))

    def col(b):
        return pl.ds(pl.multiple_of(b * BS, BS), BS)

    def body(f, carry):
        gate = jnp.zeros((rows, BS), f32)
        up = jnp.zeros((rows, BS), f32)
        hg = jnp.zeros((rows, BS), f32)
        for k in range(KG):
            ks = pl.ds(k * BS, BS)
            gate += jnp.dot(p_ref[0, :, col(gr_ref[f, k])], w_ref[f, ks, :], preferred_element_type=f32)
            up += jnp.dot(p_ref[0, :, col(ur_ref[f, k])], w_ref[slots + f, ks, :], preferred_element_type=f32)
            hg += jnp.dot(p_ref[1, :, col(dc_ref[f, k])], w_ref[2 * slots + f, ks, :], preferred_element_type=f32)
        sg = 1.0 / (1.0 + jnp.exp(-gate))
        silu = gate * sg
        hidden = (silu * up).astype(bf16)
        gg = (hg * up * sg * (1.0 + gate * (1.0 - sg))).astype(bf16)
        ug = (hg * silu).astype(bf16)
        for k in range(KG):
            ks = pl.ds(k * BS, BS)
            gt = w_ref[f, ks, :]
            ut = w_ref[slots + f, ks, :]
            dt = w_ref[2 * slots + f, ks, :]
            cd = col(dc_ref[f, k])
            cg = col(gr_ref[f, k])
            cu = col(ur_ref[f, k])
            out_acc[:, cd] += lax.dot_general(hidden, dt, nt, preferred_element_type=f32)
            in_acc[:, cg] += lax.dot_general(gg, gt, nt, preferred_element_type=f32)
            in_acc[:, cu] += lax.dot_general(ug, ut, nt, preferred_element_type=f32)
            tiles_ref[f, ks, :] = lax.dot_general(
                p_ref[0, :, cg], gg, tn, preferred_element_type=f32
            ).astype(bf16)
            tiles_ref[slots + f, ks, :] = lax.dot_general(
                p_ref[0, :, cu], ug, tn, preferred_element_type=f32
            ).astype(bf16)
            tiles_ref[2 * slots + f, ks, :] = lax.dot_general(
                p_ref[1, :, cd], hidden, tn, preferred_element_type=f32
            ).astype(bf16)
        return carry

    lax.fori_loop(0, slots, body, 0)
    panel_ref[0] = out_acc[...].astype(bf16)
    panel_ref[1] = in_acc[...].astype(bf16)


def core(panels, tiles, gate_rows, up_rows, down_columns):
    slots = gate_rows.shape[0]
    rows, width = panels.shape[1], panels.shape[2]
    smem = pl.BlockSpec(memory_space=pltpu.SMEM)
    vmem = pl.BlockSpec(memory_space=pltpu.VMEM)
    flops = 2 * rows * BS * BS * slots * KG * 9
    nbytes = 2 * (2 * panels.size + 2 * tiles.size)
    return pl.pallas_call(
        functools.partial(core_kernel, slots),
        out_shape=(
            jax.ShapeDtypeStruct((2, rows, width), jnp.bfloat16),
            jax.ShapeDtypeStruct(tiles.shape, jnp.bfloat16),
        ),
        in_specs=[smem, smem, smem, vmem, vmem],
        out_specs=(vmem, vmem),
        scratch_shapes=[
            pltpu.VMEM((rows, width), jnp.float32),
            pltpu.VMEM((rows, width), jnp.float32),
        ],
        compiler_params=pltpu.CompilerParams(vmem_limit_bytes=62 * 1024 * 1024),
        cost_estimate=pl.CostEstimate(
            flops=flops, transcendentals=rows * BS * slots, bytes_accessed=nbytes
        ),
    )(gate_rows, up_rows, down_columns, panels, tiles)


def shards(tokens, out_grad, gate_weight, up_weight, down_weight, gate_rows, up_rows, down_columns):
    owned_slots = gate_weight.shape[0]
    panels = lax.all_gather(jnp.stack([tokens, out_grad]), "col", axis=2, tiled=True)
    n_row = lax.axis_size("row")
    tiles = gather_rows(jnp.concatenate([gate_weight, up_weight, down_weight], axis=0), n_row)
    panel_part, tile_part = core(panels, tiles, gate_rows, up_rows, down_columns)
    tile_sums = lax.psum_scatter(tile_part, "row", scatter_dimension=1, tiled=True)
    panel_sums = lax.psum_scatter(panel_part, "col", scatter_dimension=2, tiled=True)
    return (
        panel_sums[0],
        panel_sums[1],
        tile_sums[:owned_slots],
        tile_sums[owned_slots : 2 * owned_slots],
        tile_sums[2 * owned_slots :],
    )


def solution(mesh):
    in_specs = (
        P("row", "col"),
        P("row", "col"),
        P("col", "row", None),
        P("col", "row", None),
        P("col", "row", None),
        P("col", None),
        P("col", None),
        P("col", None),
    )
    out_specs = (
        P("row", "col"),
        P("row", "col"),
        P("col", "row", None),
        P("col", "row", None),
        P("col", "row", None),
    )
    return jax.shard_map(shards, mesh=mesh, in_specs=in_specs, out_specs=out_specs, check_vma=False)
```

```python
import functools

import jax
import jax.numpy as jnp
from jax import lax
from jax.experimental import pallas as pl
from jax.experimental.pallas import tpu as pltpu
from jax.sharding import PartitionSpec as P

BS = 128
KG = 8
KH = 8


MESH = pl.DeviceIdType.MESH


def gather_rows_kernel(n_row, w_ref, out_ref, lsem, psend, precv, rsend, rrecv, fsend, frecv):
    me = lax.axis_index("row")
    n_chip = n_row // 2
    z = me // 2
    c = me % 2
    step_dir = 1 - 2 * c
    partner = z * 2 + (1 - c)
    nxt = ((z + step_dir + n_chip) % n_chip) * 2 + c
    prv = ((z - step_dir + n_chip) % n_chip) * 2 + c
    half = w_ref.shape[1]
    tile = 2 * half

    barrier = pltpu.get_barrier_semaphore()
    for peer in (partner, nxt, prv):
        pl.semaphore_signal(barrier, inc=1, device_id={"row": peer}, device_id_type=MESH)
    pl.semaphore_wait(barrier, 3)

    def chip_tile(p):
        return out_ref.at[:, pl.ds(pl.multiple_of(p * tile, tile), tile), :]

    own = out_ref.at[:, pl.ds(pl.multiple_of(z * tile + c * half, half), half), :]
    local = pltpu.make_async_copy(w_ref, own, lsem)
    local.start()
    swap = pltpu.make_async_remote_copy(
        src_ref=w_ref, dst_ref=own, send_sem=psend, recv_sem=precv,
        device_id={"row": partner}, device_id_type=MESH,
    )
    swap.start()
    local.wait()
    theirs = out_ref.at[:, pl.ds(pl.multiple_of(z * tile + (1 - c) * half, half), half), :]
    pltpu.make_async_remote_copy(
        src_ref=w_ref, dst_ref=theirs, send_sem=psend, recv_sem=precv,
        device_id={"row": partner}, device_id_type=MESH,
    ).wait_recv()
    swap.wait_send()

    steps = n_chip // 2
    sends = []
    fwds = []
    for s in range(1, steps + 1):
        p_send = (z - (s - 1) * step_dir + n_chip * steps) % n_chip
        p_recv = (z - s * step_dir + n_chip * steps) % n_chip
        ring = pltpu.make_async_remote_copy(
            src_ref=chip_tile(p_send), dst_ref=chip_tile(p_send),
            send_sem=rsend.at[s - 1], recv_sem=rrecv.at[s - 1],
            device_id={"row": nxt}, device_id_type=MESH,
        )
        ring.start()
        sends.append(ring)
        pltpu.make_async_remote_copy(
            src_ref=chip_tile(p_recv), dst_ref=chip_tile(p_recv),
            send_sem=rsend.at[s - 1], recv_sem=rrecv.at[s - 1],
            device_id={"row": prv}, device_id_type=MESH,
        ).wait_recv()
        if s < steps:
            fwd = pltpu.make_async_remote_copy(
                src_ref=chip_tile(p_recv), dst_ref=chip_tile(p_recv),
                send_sem=fsend.at[s - 1], recv_sem=frecv.at[s - 1],
                device_id={"row": partner}, device_id_type=MESH,
            )
            fwd.start()
            fwds.append(fwd)
    for s in range(1, steps):
        p_in = (z + s * step_dir + n_chip * steps) % n_chip
        pltpu.make_async_remote_copy(
            src_ref=chip_tile(p_in), dst_ref=chip_tile(p_in),
            send_sem=fsend.at[s - 1], recv_sem=frecv.at[s - 1],
            device_id={"row": partner}, device_id_type=MESH,
        ).wait_recv()
    for cp in sends + fwds:
        cp.wait_send()


def gather_rows(w, n_row):
    slots, half, width = w.shape
    steps = n_row // 4
    any_spec = pl.BlockSpec(memory_space=pl.ANY)
    return pl.pallas_call(
        functools.partial(gather_rows_kernel, n_row),
        out_shape=jax.ShapeDtypeStruct((slots, half * n_row, width), w.dtype),
        in_specs=[any_spec],
        out_specs=any_spec,
        scratch_shapes=[
            pltpu.SemaphoreType.DMA(()),
            pltpu.SemaphoreType.DMA(()),
            pltpu.SemaphoreType.DMA(()),
            pltpu.SemaphoreType.DMA((steps,)),
            pltpu.SemaphoreType.DMA((steps,)),
            pltpu.SemaphoreType.DMA((steps - 1,)),
            pltpu.SemaphoreType.DMA((steps - 1,)),
        ],
        compiler_params=pltpu.CompilerParams(collective_id=0, has_side_effects=True),
        cost_estimate=pl.CostEstimate(flops=0, transcendentals=0, bytes_accessed=2 * w.size * n_row),
    )(w)


def scatter_rows_kernel(n_row, x_ref, out_ref, part_buf, send_buf, recv_buf, psend, precv, rsend, rrecv):
    me = lax.axis_index("row")
    n_chip = n_row // 2
    z = me // 2
    c = me % 2
    step_dir = 1 - 2 * c
    partner = z * 2 + (1 - c)
    nxt = ((z + step_dir + n_chip) % n_chip) * 2 + c
    prv = ((z - step_dir + n_chip) % n_chip) * 2 + c
    f32 = jnp.float32

    barrier = pltpu.get_barrier_semaphore()
    for peer in (partner, nxt, prv):
        pl.semaphore_signal(barrier, inc=1, device_id={"row": peer}, device_id_type=MESH)
    pl.semaphore_wait(barrier, 3)

    swap = pltpu.make_async_remote_copy(
        src_ref=x_ref.at[:, :, 1 - c], dst_ref=part_buf, send_sem=psend, recv_sem=precv,
        device_id={"row": partner}, device_id_type=MESH,
    )
    swap.start()
    swap.wait_recv()

    def chip_part(q):
        return x_ref[:, q, c].astype(f32) + part_buf[:, q].astype(f32)

    sends = []
    for s in range(1, n_chip):
        q = (z - s * step_dir + n_chip * n_chip) % n_chip
        if s == 1:
            send_buf[s - 1] = chip_part(q)
        else:
            send_buf[s - 1] = recv_buf[s - 2] + chip_part(q)
        ring = pltpu.make_async_remote_copy(
            src_ref=send_buf.at[s - 1], dst_ref=recv_buf.at[s - 1],
            send_sem=rsend.at[s - 1], recv_sem=rrecv.at[s - 1],
            device_id={"row": nxt}, device_id_type=MESH,
        )
        ring.start()
        sends.append(ring)
        ring.wait_recv()
    out_ref[...] = (recv_buf[n_chip - 2] + chip_part(z)).astype(out_ref.dtype)
    swap.wait_send()
    for cp in sends:
        cp.wait_send()


def scatter_rows(x, n_row):
    slots, height, width = x.shape
    n_chip = n_row // 2
    half = height // n_row
    x5 = x.reshape(slots, n_chip, 2, half, width)
    vmem = pl.BlockSpec(memory_space=pltpu.VMEM)
    return pl.pallas_call(
        functools.partial(scatter_rows_kernel, n_row),
        out_shape=jax.ShapeDtypeStruct((slots, half, width), x.dtype),
        in_specs=[vmem],
        out_specs=vmem,
        scratch_shapes=[
            pltpu.VMEM((slots, n_chip, half, width), x.dtype),
            pltpu.VMEM((n_chip - 1, slots, half, width), jnp.float32),
            pltpu.VMEM((n_chip - 1, slots, half, width), jnp.float32),
            pltpu.SemaphoreType.DMA(()),
            pltpu.SemaphoreType.DMA(()),
            pltpu.SemaphoreType.DMA((n_chip - 1,)),
            pltpu.SemaphoreType.DMA((n_chip - 1,)),
        ],
        compiler_params=pltpu.CompilerParams(
            collective_id=1, has_side_effects=True, vmem_limit_bytes=48 * 1024 * 1024
        ),
        cost_estimate=pl.CostEstimate(
            flops=x.size, transcendentals=0, bytes_accessed=4 * x.size
        ),
    )(x5)


def core_kernel(slots, gr_ref, ur_ref, dc_ref, p_ref, w_ref, panel_ref, tiles_ref, out_acc, in_acc):
    out_acc[...] = jnp.zeros_like(out_acc)
    in_acc[...] = jnp.zeros_like(in_acc)
    f32 = jnp.float32
    bf16 = jnp.bfloat16
    rows = p_ref.shape[1]
    tn = (((0,), (0,)), ((), ()))
    nt = (((1,), (1,)), ((), ()))

    def col(b):
        return pl.ds(pl.multiple_of(b * BS, BS), BS)

    def body(f, carry):
        gate = jnp.zeros((rows, BS), f32)
        up = jnp.zeros((rows, BS), f32)
        hg = jnp.zeros((rows, BS), f32)
        for k in range(KG):
            ks = pl.ds(k * BS, BS)
            gate += jnp.dot(p_ref[0, :, col(gr_ref[f, k])], w_ref[f, ks, :], preferred_element_type=f32)
            up += jnp.dot(p_ref[0, :, col(ur_ref[f, k])], w_ref[slots + f, ks, :], preferred_element_type=f32)
            hg += jnp.dot(p_ref[1, :, col(dc_ref[f, k])], w_ref[2 * slots + f, ks, :], preferred_element_type=f32)
        sg = 1.0 / (1.0 + jnp.exp(-gate))
        silu = gate * sg
        hidden = (silu * up).astype(bf16)
        gg = (hg * up * sg * (1.0 + gate * (1.0 - sg))).astype(bf16)
        ug = (hg * silu).astype(bf16)
        for k in range(KG):
            ks = pl.ds(k * BS, BS)
            gt = w_ref[f, ks, :]
            ut = w_ref[slots + f, ks, :]
            dt = w_ref[2 * slots + f, ks, :]
            cd = col(dc_ref[f, k])
            cg = col(gr_ref[f, k])
            cu = col(ur_ref[f, k])
            out_acc[:, cd] += lax.dot_general(hidden, dt, nt, preferred_element_type=f32)
            in_acc[:, cg] += lax.dot_general(gg, gt, nt, preferred_element_type=f32)
            in_acc[:, cu] += lax.dot_general(ug, ut, nt, preferred_element_type=f32)
            tiles_ref[f, ks, :] = lax.dot_general(
                p_ref[0, :, cg], gg, tn, preferred_element_type=f32
            ).astype(bf16)
            tiles_ref[slots + f, ks, :] = lax.dot_general(
                p_ref[0, :, cu], ug, tn, preferred_element_type=f32
            ).astype(bf16)
            tiles_ref[2 * slots + f, ks, :] = lax.dot_general(
                p_ref[1, :, cd], hidden, tn, preferred_element_type=f32
            ).astype(bf16)
        return carry

    lax.fori_loop(0, slots, body, 0)
    panel_ref[0] = out_acc[...].astype(bf16)
    panel_ref[1] = in_acc[...].astype(bf16)


def core(panels, tiles, gate_rows, up_rows, down_columns):
    slots = gate_rows.shape[0]
    rows, width = panels.shape[1], panels.shape[2]
    smem = pl.BlockSpec(memory_space=pltpu.SMEM)
    vmem = pl.BlockSpec(memory_space=pltpu.VMEM)
    flops = 2 * rows * BS * BS * slots * KG * 9
    nbytes = 2 * (2 * panels.size + 2 * tiles.size)
    return pl.pallas_call(
        functools.partial(core_kernel, slots),
        out_shape=(
            jax.ShapeDtypeStruct((2, rows, width), jnp.bfloat16),
            jax.ShapeDtypeStruct(tiles.shape, jnp.bfloat16),
        ),
        in_specs=[smem, smem, smem, vmem, vmem],
        out_specs=(vmem, vmem),
        scratch_shapes=[
            pltpu.VMEM((rows, width), jnp.float32),
            pltpu.VMEM((rows, width), jnp.float32),
        ],
        compiler_params=pltpu.CompilerParams(vmem_limit_bytes=62 * 1024 * 1024),
        cost_estimate=pl.CostEstimate(
            flops=flops, transcendentals=rows * BS * slots, bytes_accessed=nbytes
        ),
    )(gate_rows, up_rows, down_columns, panels, tiles)


def shards(tokens, out_grad, gate_weight, up_weight, down_weight, gate_rows, up_rows, down_columns):
    owned_slots = gate_weight.shape[0]
    panels = lax.all_gather(jnp.stack([tokens, out_grad]), "col", axis=2, tiled=True)
    n_row = lax.axis_size("row")
    tiles = gather_rows(jnp.concatenate([gate_weight, up_weight, down_weight], axis=0), n_row)
    panel_part, tile_part = core(panels, tiles, gate_rows, up_rows, down_columns)
    tile_sums = scatter_rows(tile_part, n_row)
    panel_sums = lax.psum_scatter(panel_part, "col", scatter_dimension=2, tiled=True)
    return (
        panel_sums[0],
        panel_sums[1],
        tile_sums[:owned_slots],
        tile_sums[owned_slots : 2 * owned_slots],
        tile_sums[2 * owned_slots :],
    )


def solution(mesh):
    in_specs = (
        P("row", "col"),
        P("row", "col"),
        P("col", "row", None),
        P("col", "row", None),
        P("col", "row", None),
        P("col", None),
        P("col", None),
        P("col", None),
    )
    out_specs = (
        P("row", "col"),
        P("row", "col"),
        P("col", "row", None),
        P("col", "row", None),
        P("col", "row", None),
    )
    return jax.shard_map(shards, mesh=mesh, in_specs=in_specs, out_specs=out_specs, check_vma=False)
```

```python
import functools

import jax
import jax.numpy as jnp
from jax import lax
from jax.experimental import pallas as pl
from jax.experimental.pallas import tpu as pltpu
from jax.sharding import PartitionSpec as P

BS = 128
KG = 8
KH = 8


MESH = pl.DeviceIdType.MESH


def gather_rows_kernel(n_row, w_ref, out_ref, lsem, psend, precv, rsend, rrecv, fsend, frecv):
    me = lax.axis_index("row")
    n_chip = n_row // 2
    z = me // 2
    c = me % 2
    step_dir = 1 - 2 * c
    partner = z * 2 + (1 - c)
    nxt = ((z + step_dir + n_chip) % n_chip) * 2 + c
    prv = ((z - step_dir + n_chip) % n_chip) * 2 + c
    half = w_ref.shape[1]
    tile = 2 * half

    barrier = pltpu.get_barrier_semaphore()
    for peer in (partner, nxt, prv):
        pl.semaphore_signal(barrier, inc=1, device_id={"row": peer}, device_id_type=MESH)
    pl.semaphore_wait(barrier, 3)

    def chip_tile(p):
        return out_ref.at[:, pl.ds(pl.multiple_of(p * tile, tile), tile), :]

    own = out_ref.at[:, pl.ds(pl.multiple_of(z * tile + c * half, half), half), :]
    local = pltpu.make_async_copy(w_ref, own, lsem)
    local.start()
    swap = pltpu.make_async_remote_copy(
        src_ref=w_ref, dst_ref=own, send_sem=psend, recv_sem=precv,
        device_id={"row": partner}, device_id_type=MESH,
    )
    swap.start()
    local.wait()
    theirs = out_ref.at[:, pl.ds(pl.multiple_of(z * tile + (1 - c) * half, half), half), :]
    pltpu.make_async_remote_copy(
        src_ref=w_ref, dst_ref=theirs, send_sem=psend, recv_sem=precv,
        device_id={"row": partner}, device_id_type=MESH,
    ).wait_recv()
    swap.wait_send()

    steps = n_chip // 2
    sends = []
    fwds = []
    for s in range(1, steps + 1):
        p_send = (z - (s - 1) * step_dir + n_chip * steps) % n_chip
        p_recv = (z - s * step_dir + n_chip * steps) % n_chip
        ring = pltpu.make_async_remote_copy(
            src_ref=chip_tile(p_send), dst_ref=chip_tile(p_send),
            send_sem=rsend.at[s - 1], recv_sem=rrecv.at[s - 1],
            device_id={"row": nxt}, device_id_type=MESH,
        )
        ring.start()
        sends.append(ring)
        pltpu.make_async_remote_copy(
            src_ref=chip_tile(p_recv), dst_ref=chip_tile(p_recv),
            send_sem=rsend.at[s - 1], recv_sem=rrecv.at[s - 1],
            device_id={"row": prv}, device_id_type=MESH,
        ).wait_recv()
        if s < steps:
            fwd = pltpu.make_async_remote_copy(
                src_ref=chip_tile(p_recv), dst_ref=chip_tile(p_recv),
                send_sem=fsend.at[s - 1], recv_sem=frecv.at[s - 1],
                device_id={"row": partner}, device_id_type=MESH,
            )
            fwd.start()
            fwds.append(fwd)
    for s in range(1, steps):
        p_in = (z + s * step_dir + n_chip * steps) % n_chip
        pltpu.make_async_remote_copy(
            src_ref=chip_tile(p_in), dst_ref=chip_tile(p_in),
            send_sem=fsend.at[s - 1], recv_sem=frecv.at[s - 1],
            device_id={"row": partner}, device_id_type=MESH,
        ).wait_recv()
    for cp in sends + fwds:
        cp.wait_send()


def gather_rows(w, n_row):
    slots, half, width = w.shape
    steps = n_row // 4
    any_spec = pl.BlockSpec(memory_space=pl.ANY)
    return pl.pallas_call(
        functools.partial(gather_rows_kernel, n_row),
        out_shape=jax.ShapeDtypeStruct((slots, half * n_row, width), w.dtype),
        in_specs=[any_spec],
        out_specs=any_spec,
        scratch_shapes=[
            pltpu.SemaphoreType.DMA(()),
            pltpu.SemaphoreType.DMA(()),
            pltpu.SemaphoreType.DMA(()),
            pltpu.SemaphoreType.DMA((steps,)),
            pltpu.SemaphoreType.DMA((steps,)),
            pltpu.SemaphoreType.DMA((steps - 1,)),
            pltpu.SemaphoreType.DMA((steps - 1,)),
        ],
        compiler_params=pltpu.CompilerParams(collective_id=0, has_side_effects=True),
        cost_estimate=pl.CostEstimate(flops=0, transcendentals=0, bytes_accessed=2 * w.size * n_row),
    )(w)


def scatter_rows_kernel(n_row, x_ref, out_ref, part_buf, send_buf, recv_buf, psend, precv, rsend, rrecv):
    me = lax.axis_index("row")
    n_chip = n_row // 2
    z = me // 2
    c = me % 2
    step_dir = 1 - 2 * c
    partner = z * 2 + (1 - c)
    nxt = ((z + step_dir + n_chip) % n_chip) * 2 + c
    prv = ((z - step_dir + n_chip) % n_chip) * 2 + c
    f32 = jnp.float32

    barrier = pltpu.get_barrier_semaphore()
    for peer in (partner, nxt, prv):
        pl.semaphore_signal(barrier, inc=1, device_id={"row": peer}, device_id_type=MESH)
    pl.semaphore_wait(barrier, 3)

    swap = pltpu.make_async_remote_copy(
        src_ref=x_ref.at[:, :, 1 - c], dst_ref=part_buf, send_sem=psend, recv_sem=precv,
        device_id={"row": partner}, device_id_type=MESH,
    )
    swap.start()
    swap.wait_recv()

    def chip_part(q):
        return x_ref[:, q, c].astype(f32) + part_buf[:, q].astype(f32)

    sends = []
    for s in range(1, n_chip):
        q = (z - s * step_dir + n_chip * n_chip) % n_chip
        if s == 1:
            send_buf[s - 1] = chip_part(q)
        else:
            send_buf[s - 1] = recv_buf[s - 2] + chip_part(q)
        ring = pltpu.make_async_remote_copy(
            src_ref=send_buf.at[s - 1], dst_ref=recv_buf.at[s - 1],
            send_sem=rsend.at[s - 1], recv_sem=rrecv.at[s - 1],
            device_id={"row": nxt}, device_id_type=MESH,
        )
        ring.start()
        sends.append(ring)
        ring.wait_recv()
    out_ref[...] = (recv_buf[n_chip - 2] + chip_part(z)).astype(out_ref.dtype)
    swap.wait_send()
    for cp in sends:
        cp.wait_send()


def scatter_rows(x, n_row):
    slots, height, width = x.shape
    n_chip = n_row // 2
    half = height // n_row
    x5 = x.reshape(slots, n_chip, 2, half, width)
    vmem = pl.BlockSpec(memory_space=pltpu.VMEM)
    return pl.pallas_call(
        functools.partial(scatter_rows_kernel, n_row),
        out_shape=jax.ShapeDtypeStruct((slots, half, width), x.dtype),
        in_specs=[vmem],
        out_specs=vmem,
        scratch_shapes=[
            pltpu.VMEM((slots, n_chip, half, width), x.dtype),
            pltpu.VMEM((n_chip - 1, slots, half, width), jnp.float32),
            pltpu.VMEM((n_chip - 1, slots, half, width), jnp.float32),
            pltpu.SemaphoreType.DMA(()),
            pltpu.SemaphoreType.DMA(()),
            pltpu.SemaphoreType.DMA((n_chip - 1,)),
            pltpu.SemaphoreType.DMA((n_chip - 1,)),
        ],
        compiler_params=pltpu.CompilerParams(
            collective_id=1, has_side_effects=True, vmem_limit_bytes=48 * 1024 * 1024
        ),
        cost_estimate=pl.CostEstimate(
            flops=x.size, transcendentals=0, bytes_accessed=4 * x.size
        ),
    )(x5)


def core_kernel(slots, gr_ref, ur_ref, dc_ref, p_ref, w_ref, panel_ref, tiles_ref, out_acc, in_acc):
    out_acc[...] = jnp.zeros_like(out_acc)
    in_acc[...] = jnp.zeros_like(in_acc)
    f32 = jnp.float32
    bf16 = jnp.bfloat16
    peers, _, rows, chunk = p_ref.shape
    per = chunk // BS
    tn = (((0,), (0,)), ((), ()))
    nt = (((1,), (1,)), ((), ()))

    def col(b):
        return pl.ds(pl.multiple_of(b * BS, BS), BS)

    def block(which, b):
        return p_ref[b // per, which, :, pl.ds(pl.multiple_of((b % per) * BS, BS), BS)]

    def body(f, carry):
        gate = jnp.zeros((rows, BS), f32)
        up = jnp.zeros((rows, BS), f32)
        hg = jnp.zeros((rows, BS), f32)
        for k in range(KG):
            ks = pl.ds(k * BS, BS)
            gate += jnp.dot(block(0, gr_ref[f, k]), w_ref[f, ks, :], preferred_element_type=f32)
            up += jnp.dot(block(0, ur_ref[f, k]), w_ref[slots + f, ks, :], preferred_element_type=f32)
            hg += jnp.dot(block(1, dc_ref[f, k]), w_ref[2 * slots + f, ks, :], preferred_element_type=f32)
        sg = 1.0 / (1.0 + jnp.exp(-gate))
        silu = gate * sg
        hidden = (silu * up).astype(bf16)
        gg = (hg * up * sg * (1.0 + gate * (1.0 - sg))).astype(bf16)
        ug = (hg * silu).astype(bf16)
        for k in range(KG):
            ks = pl.ds(k * BS, BS)
            gt = w_ref[f, ks, :]
            ut = w_ref[slots + f, ks, :]
            dt = w_ref[2 * slots + f, ks, :]
            bd = dc_ref[f, k]
            bg = gr_ref[f, k]
            bu = ur_ref[f, k]
            out_acc[:, col(bd)] += lax.dot_general(hidden, dt, nt, preferred_element_type=f32)
            in_acc[:, col(bg)] += lax.dot_general(gg, gt, nt, preferred_element_type=f32)
            in_acc[:, col(bu)] += lax.dot_general(ug, ut, nt, preferred_element_type=f32)
            tiles_ref[f, ks, :] = lax.dot_general(
                block(0, bg), gg, tn, preferred_element_type=f32
            ).astype(bf16)
            tiles_ref[slots + f, ks, :] = lax.dot_general(
                block(0, bu), ug, tn, preferred_element_type=f32
            ).astype(bf16)
            tiles_ref[2 * slots + f, ks, :] = lax.dot_general(
                block(1, bd), hidden, tn, preferred_element_type=f32
            ).astype(bf16)
        return carry

    lax.fori_loop(0, slots, body, 0)
    for j in range(peers):
        cs = pl.ds(j * chunk, chunk)
        panel_ref[j, 0] = out_acc[:, cs].astype(bf16)
        panel_ref[j, 1] = in_acc[:, cs].astype(bf16)


def core(panels, tiles, gate_rows, up_rows, down_columns):
    slots = gate_rows.shape[0]
    peers, _, rows, chunk = panels.shape
    width = peers * chunk
    smem = pl.BlockSpec(memory_space=pltpu.SMEM)
    vmem = pl.BlockSpec(memory_space=pltpu.VMEM)
    flops = 2 * rows * BS * BS * slots * KG * 9
    nbytes = 2 * (2 * panels.size + 2 * tiles.size)
    return pl.pallas_call(
        functools.partial(core_kernel, slots),
        out_shape=(
            jax.ShapeDtypeStruct(panels.shape, jnp.bfloat16),
            jax.ShapeDtypeStruct(tiles.shape, jnp.bfloat16),
        ),
        in_specs=[smem, smem, smem, vmem, vmem],
        out_specs=(vmem, vmem),
        scratch_shapes=[
            pltpu.VMEM((rows, width), jnp.float32),
            pltpu.VMEM((rows, width), jnp.float32),
        ],
        compiler_params=pltpu.CompilerParams(vmem_limit_bytes=62 * 1024 * 1024),
        cost_estimate=pl.CostEstimate(
            flops=flops, transcendentals=rows * BS * slots, bytes_accessed=nbytes
        ),
    )(gate_rows, up_rows, down_columns, panels, tiles)


def shards(tokens, out_grad, gate_weight, up_weight, down_weight, gate_rows, up_rows, down_columns):
    owned_slots = gate_weight.shape[0]
    panels = lax.all_gather(jnp.stack([tokens, out_grad]), "col", axis=0)
    n_row = lax.axis_size("row")
    tiles = gather_rows(jnp.concatenate([gate_weight, up_weight, down_weight], axis=0), n_row)
    panel_part, tile_part = core(panels, tiles, gate_rows, up_rows, down_columns)
    tile_sums = scatter_rows(tile_part, n_row)
    peers, _, rows, chunk = panel_part.shape
    panel_sums = lax.psum_scatter(
        panel_part.reshape(peers * 2 * rows, chunk), "col", scatter_dimension=0, tiled=True
    ).reshape(2, rows, chunk)
    return (
        panel_sums[0],
        panel_sums[1],
        tile_sums[:owned_slots],
        tile_sums[owned_slots : 2 * owned_slots],
        tile_sums[2 * owned_slots :],
    )


def solution(mesh):
    in_specs = (
        P("row", "col"),
        P("row", "col"),
        P("col", "row", None),
        P("col", "row", None),
        P("col", "row", None),
        P("col", None),
        P("col", None),
        P("col", None),
    )
    out_specs = (
        P("row", "col"),
        P("row", "col"),
        P("col", "row", None),
        P("col", "row", None),
        P("col", "row", None),
    )
    return jax.shard_map(shards, mesh=mesh, in_specs=in_specs, out_specs=out_specs, check_vma=False)
```

```python
import functools

import jax
import jax.numpy as jnp
from jax import lax
from jax.experimental import pallas as pl
from jax.experimental.pallas import tpu as pltpu
from jax.sharding import PartitionSpec as P

BS = 128
KG = 8
KH = 8


MESH = pl.DeviceIdType.MESH


def gather_rows_kernel(n_row, w_ref, out_ref, lsem, psend, precv, rsend, rrecv, fsend, frecv):
    me = lax.axis_index("row")
    n_chip = n_row // 2
    z = me // 2
    c = me % 2
    step_dir = 1 - 2 * c
    partner = z * 2 + (1 - c)
    nxt = ((z + step_dir + n_chip) % n_chip) * 2 + c
    prv = ((z - step_dir + n_chip) % n_chip) * 2 + c
    half = w_ref.shape[1]
    tile = 2 * half

    barrier = pltpu.get_barrier_semaphore()
    for peer in (partner, nxt, prv):
        pl.semaphore_signal(barrier, inc=1, device_id={"row": peer}, device_id_type=MESH)
    pl.semaphore_wait(barrier, 3)

    def chip_tile(p):
        return out_ref.at[:, pl.ds(pl.multiple_of(p * tile, tile), tile), :]

    own = out_ref.at[:, pl.ds(pl.multiple_of(z * tile + c * half, half), half), :]
    local = pltpu.make_async_copy(w_ref, own, lsem)
    local.start()
    swap = pltpu.make_async_remote_copy(
        src_ref=w_ref, dst_ref=own, send_sem=psend, recv_sem=precv,
        device_id={"row": partner}, device_id_type=MESH,
    )
    swap.start()
    local.wait()
    theirs = out_ref.at[:, pl.ds(pl.multiple_of(z * tile + (1 - c) * half, half), half), :]
    pltpu.make_async_remote_copy(
        src_ref=w_ref, dst_ref=theirs, send_sem=psend, recv_sem=precv,
        device_id={"row": partner}, device_id_type=MESH,
    ).wait_recv()
    swap.wait_send()

    steps = n_chip // 2
    sends = []
    fwds = []
    for s in range(1, steps + 1):
        p_send = (z - (s - 1) * step_dir + n_chip * steps) % n_chip
        p_recv = (z - s * step_dir + n_chip * steps) % n_chip
        ring = pltpu.make_async_remote_copy(
            src_ref=chip_tile(p_send), dst_ref=chip_tile(p_send),
            send_sem=rsend.at[s - 1], recv_sem=rrecv.at[s - 1],
            device_id={"row": nxt}, device_id_type=MESH,
        )
        ring.start()
        sends.append(ring)
        pltpu.make_async_remote_copy(
            src_ref=chip_tile(p_recv), dst_ref=chip_tile(p_recv),
            send_sem=rsend.at[s - 1], recv_sem=rrecv.at[s - 1],
            device_id={"row": prv}, device_id_type=MESH,
        ).wait_recv()
        if s < steps:
            fwd = pltpu.make_async_remote_copy(
                src_ref=chip_tile(p_recv), dst_ref=chip_tile(p_recv),
                send_sem=fsend.at[s - 1], recv_sem=frecv.at[s - 1],
                device_id={"row": partner}, device_id_type=MESH,
            )
            fwd.start()
            fwds.append(fwd)
    for s in range(1, steps):
        p_in = (z + s * step_dir + n_chip * steps) % n_chip
        pltpu.make_async_remote_copy(
            src_ref=chip_tile(p_in), dst_ref=chip_tile(p_in),
            send_sem=fsend.at[s - 1], recv_sem=frecv.at[s - 1],
            device_id={"row": partner}, device_id_type=MESH,
        ).wait_recv()
    for cp in sends + fwds:
        cp.wait_send()


def gather_rows(w, n_row):
    slots, half, width = w.shape
    steps = n_row // 4
    any_spec = pl.BlockSpec(memory_space=pl.ANY)
    return pl.pallas_call(
        functools.partial(gather_rows_kernel, n_row),
        out_shape=jax.ShapeDtypeStruct((slots, half * n_row, width), w.dtype),
        in_specs=[any_spec],
        out_specs=any_spec,
        scratch_shapes=[
            pltpu.SemaphoreType.DMA(()),
            pltpu.SemaphoreType.DMA(()),
            pltpu.SemaphoreType.DMA(()),
            pltpu.SemaphoreType.DMA((steps,)),
            pltpu.SemaphoreType.DMA((steps,)),
            pltpu.SemaphoreType.DMA((steps - 1,)),
            pltpu.SemaphoreType.DMA((steps - 1,)),
        ],
        compiler_params=pltpu.CompilerParams(collective_id=0, has_side_effects=True),
        cost_estimate=pl.CostEstimate(flops=0, transcendentals=0, bytes_accessed=2 * w.size * n_row),
    )(w)


def scatter_rows_kernel(n_row, x_ref, out_ref, part_buf, send_buf, recv_buf, psend, precv, rsend, rrecv):
    me = lax.axis_index("row")
    n_chip = n_row // 2
    z = me // 2
    c = me % 2
    step_dir = 1 - 2 * c
    partner = z * 2 + (1 - c)
    nxt = ((z + step_dir + n_chip) % n_chip) * 2 + c
    prv = ((z - step_dir + n_chip) % n_chip) * 2 + c
    f32 = jnp.float32

    barrier = pltpu.get_barrier_semaphore()
    for peer in (partner, nxt, prv):
        pl.semaphore_signal(barrier, inc=1, device_id={"row": peer}, device_id_type=MESH)
    pl.semaphore_wait(barrier, 3)

    swap = pltpu.make_async_remote_copy(
        src_ref=x_ref.at[:, :, 1 - c], dst_ref=part_buf, send_sem=psend, recv_sem=precv,
        device_id={"row": partner}, device_id_type=MESH,
    )
    swap.start()
    swap.wait_recv()

    def chip_part(q):
        return x_ref[:, q, c].astype(f32) + part_buf[:, q].astype(f32)

    sends = []
    for s in range(1, n_chip):
        q = (z - s * step_dir + n_chip * n_chip) % n_chip
        if s == 1:
            send_buf[s - 1] = chip_part(q)
        else:
            send_buf[s - 1] = recv_buf[s - 2] + chip_part(q)
        ring = pltpu.make_async_remote_copy(
            src_ref=send_buf.at[s - 1], dst_ref=recv_buf.at[s - 1],
            send_sem=rsend.at[s - 1], recv_sem=rrecv.at[s - 1],
            device_id={"row": nxt}, device_id_type=MESH,
        )
        ring.start()
        sends.append(ring)
        ring.wait_recv()
    out_ref[...] = (recv_buf[n_chip - 2] + chip_part(z)).astype(out_ref.dtype)
    swap.wait_send()
    for cp in sends:
        cp.wait_send()


def scatter_rows(x, n_row):
    slots, height, width = x.shape
    n_chip = n_row // 2
    half = height // n_row
    x5 = x.reshape(slots, n_chip, 2, half, width)
    vmem = pl.BlockSpec(memory_space=pltpu.VMEM)
    return pl.pallas_call(
        functools.partial(scatter_rows_kernel, n_row),
        out_shape=jax.ShapeDtypeStruct((slots, half, width), x.dtype),
        in_specs=[vmem],
        out_specs=vmem,
        scratch_shapes=[
            pltpu.VMEM((slots, n_chip, half, width), x.dtype),
            pltpu.VMEM((n_chip - 1, slots, half, width), jnp.float32),
            pltpu.VMEM((n_chip - 1, slots, half, width), jnp.float32),
            pltpu.SemaphoreType.DMA(()),
            pltpu.SemaphoreType.DMA(()),
            pltpu.SemaphoreType.DMA((n_chip - 1,)),
            pltpu.SemaphoreType.DMA((n_chip - 1,)),
        ],
        compiler_params=pltpu.CompilerParams(
            collective_id=1, has_side_effects=True, vmem_limit_bytes=48 * 1024 * 1024
        ),
        cost_estimate=pl.CostEstimate(
            flops=x.size, transcendentals=0, bytes_accessed=4 * x.size
        ),
    )(x5)


def core_kernel(slots, gr_ref, ur_ref, dc_ref, p_ref, w_ref, panel_ref, tiles_ref, out_acc, in_acc):
    out_acc[...] = jnp.zeros_like(out_acc)
    in_acc[...] = jnp.zeros_like(in_acc)
    f32 = jnp.float32
    bf16 = jnp.bfloat16
    peers, _, rows, chunk = p_ref.shape
    per = chunk // BS
    tn = (((0,), (0,)), ((), ()))
    nt = (((1,), (1,)), ((), ()))

    def col(b):
        return pl.ds(pl.multiple_of(b * BS, BS), BS)

    def block(which, b):
        return p_ref[b // per, which, :, pl.ds(pl.multiple_of((b % per) * BS, BS), BS)]

    def body(f, carry):
        gate = jnp.zeros((rows, BS), f32)
        up = jnp.zeros((rows, BS), f32)
        hg = jnp.zeros((rows, BS), f32)
        for k in range(KG):
            ks = pl.ds(k * BS, BS)
            gate += jnp.dot(block(0, gr_ref[f, k]), w_ref[f, ks, :], preferred_element_type=f32)
            up += jnp.dot(block(0, ur_ref[f, k]), w_ref[slots + f, ks, :], preferred_element_type=f32)
            hg += jnp.dot(block(1, dc_ref[f, k]), w_ref[2 * slots + f, ks, :], preferred_element_type=f32)
        sg = 1.0 / (1.0 + jnp.exp(-gate))
        silu = gate * sg
        hidden = (silu * up).astype(bf16)
        gg = (hg * up * sg * (1.0 + gate * (1.0 - sg))).astype(bf16)
        ug = (hg * silu).astype(bf16)
        for k in range(KG):
            ks = pl.ds(k * BS, BS)
            gt = w_ref[f, ks, :]
            ut = w_ref[slots + f, ks, :]
            dt = w_ref[2 * slots + f, ks, :]
            bd = dc_ref[f, k]
            bg = gr_ref[f, k]
            bu = ur_ref[f, k]
            out_acc[:, col(bd)] += lax.dot_general(hidden, dt, nt, preferred_element_type=f32)
            in_acc[:, col(bg)] += lax.dot_general(gg, gt, nt, preferred_element_type=f32)
            in_acc[:, col(bu)] += lax.dot_general(ug, ut, nt, preferred_element_type=f32)
            tiles_ref[f, ks, :] = lax.dot_general(
                block(0, bg), gg, tn, preferred_element_type=f32
            ).astype(bf16)
            tiles_ref[slots + f, ks, :] = lax.dot_general(
                block(0, bu), ug, tn, preferred_element_type=f32
            ).astype(bf16)
            tiles_ref[2 * slots + f, ks, :] = lax.dot_general(
                block(1, bd), hidden, tn, preferred_element_type=f32
            ).astype(bf16)
        return carry

    lax.fori_loop(0, slots, body, 0)
    for j in range(peers):
        cs = pl.ds(j * chunk, chunk)
        panel_ref[j, 0] = out_acc[:, cs].astype(bf16)
        panel_ref[j, 1] = in_acc[:, cs].astype(bf16)


def core(panels, tiles, gate_rows, up_rows, down_columns):
    slots = gate_rows.shape[0]
    peers, _, rows, chunk = panels.shape
    width = peers * chunk
    smem = pl.BlockSpec(memory_space=pltpu.SMEM)
    vmem = pl.BlockSpec(memory_space=pltpu.VMEM)
    flops = 2 * rows * BS * BS * slots * KG * 9
    nbytes = 2 * (2 * panels.size + 2 * tiles.size)
    return pl.pallas_call(
        functools.partial(core_kernel, slots),
        out_shape=(
            jax.ShapeDtypeStruct(panels.shape, jnp.bfloat16),
            jax.ShapeDtypeStruct(tiles.shape, jnp.bfloat16),
        ),
        in_specs=[smem, smem, smem, vmem, vmem],
        out_specs=(vmem, vmem),
        scratch_shapes=[
            pltpu.VMEM((rows, width), jnp.float32),
            pltpu.VMEM((rows, width), jnp.float32),
        ],
        compiler_params=pltpu.CompilerParams(vmem_limit_bytes=62 * 1024 * 1024),
        cost_estimate=pl.CostEstimate(
            flops=flops, transcendentals=rows * BS * slots, bytes_accessed=nbytes
        ),
    )(gate_rows, up_rows, down_columns, panels, tiles)


def shards(tokens, out_grad, gate_weight, up_weight, down_weight, gate_rows, up_rows, down_columns):
    owned_slots = gate_weight.shape[0]
    panels = lax.all_gather(jnp.stack([tokens, out_grad]), "col", axis=0)
    n_row = lax.axis_size("row")
    tiles = gather_rows(jnp.concatenate([gate_weight, up_weight, down_weight], axis=0), n_row)
    panel_part, tile_part = core(panels, tiles, gate_rows, up_rows, down_columns)
    tile_sums = scatter_rows(tile_part, n_row)
    received = lax.all_to_all(panel_part, "col", 0, 0, tiled=True)
    panel_sums = jnp.sum(received.astype(jnp.float32), axis=0).astype(jnp.bfloat16)
    return (
        panel_sums[0],
        panel_sums[1],
        tile_sums[:owned_slots],
        tile_sums[owned_slots : 2 * owned_slots],
        tile_sums[2 * owned_slots :],
    )


def solution(mesh):
    in_specs = (
        P("row", "col"),
        P("row", "col"),
        P("col", "row", None),
        P("col", "row", None),
        P("col", "row", None),
        P("col", None),
        P("col", None),
        P("col", None),
    )
    out_specs = (
        P("row", "col"),
        P("row", "col"),
        P("col", "row", None),
        P("col", "row", None),
        P("col", "row", None),
    )
    return jax.shard_map(shards, mesh=mesh, in_specs=in_specs, out_specs=out_specs, check_vma=False)
```

```python
import functools

import jax
import jax.numpy as jnp
from jax import lax
from jax.experimental import pallas as pl
from jax.experimental.pallas import tpu as pltpu
from jax.sharding import PartitionSpec as P

BS = 128
KG = 8
KH = 8


MESH = pl.DeviceIdType.MESH


def gather_rows_kernel(n_row, w_ref, out_ref, lsem, psend, precv, rsend, rrecv, fsend, frecv):
    me = lax.axis_index("row")
    n_chip = n_row // 2
    z = me // 2
    c = me % 2
    step_dir = 1 - 2 * c
    partner = z * 2 + (1 - c)
    nxt = ((z + step_dir + n_chip) % n_chip) * 2 + c
    prv = ((z - step_dir + n_chip) % n_chip) * 2 + c
    half = w_ref.shape[1]
    tile = 2 * half

    barrier = pltpu.get_barrier_semaphore()
    for peer in (partner, nxt, prv):
        pl.semaphore_signal(barrier, inc=1, device_id={"row": peer}, device_id_type=MESH)
    pl.semaphore_wait(barrier, 3)

    def chip_tile(p):
        return out_ref.at[:, pl.ds(pl.multiple_of(p * tile, tile), tile), :]

    own = out_ref.at[:, pl.ds(pl.multiple_of(z * tile + c * half, half), half), :]
    local = pltpu.make_async_copy(w_ref, own, lsem)
    local.start()
    swap = pltpu.make_async_remote_copy(
        src_ref=w_ref, dst_ref=own, send_sem=psend, recv_sem=precv,
        device_id={"row": partner}, device_id_type=MESH,
    )
    swap.start()
    local.wait()
    theirs = out_ref.at[:, pl.ds(pl.multiple_of(z * tile + (1 - c) * half, half), half), :]
    pltpu.make_async_remote_copy(
        src_ref=w_ref, dst_ref=theirs, send_sem=psend, recv_sem=precv,
        device_id={"row": partner}, device_id_type=MESH,
    ).wait_recv()
    swap.wait_send()

    steps = n_chip // 2
    sends = []
    fwds = []
    for s in range(1, steps + 1):
        p_send = (z - (s - 1) * step_dir + n_chip * steps) % n_chip
        p_recv = (z - s * step_dir + n_chip * steps) % n_chip
        ring = pltpu.make_async_remote_copy(
            src_ref=chip_tile(p_send), dst_ref=chip_tile(p_send),
            send_sem=rsend.at[s - 1], recv_sem=rrecv.at[s - 1],
            device_id={"row": nxt}, device_id_type=MESH,
        )
        ring.start()
        sends.append(ring)
        pltpu.make_async_remote_copy(
            src_ref=chip_tile(p_recv), dst_ref=chip_tile(p_recv),
            send_sem=rsend.at[s - 1], recv_sem=rrecv.at[s - 1],
            device_id={"row": prv}, device_id_type=MESH,
        ).wait_recv()
        if s < steps:
            fwd = pltpu.make_async_remote_copy(
                src_ref=chip_tile(p_recv), dst_ref=chip_tile(p_recv),
                send_sem=fsend.at[s - 1], recv_sem=frecv.at[s - 1],
                device_id={"row": partner}, device_id_type=MESH,
            )
            fwd.start()
            fwds.append(fwd)
    for s in range(1, steps):
        p_in = (z + s * step_dir + n_chip * steps) % n_chip
        pltpu.make_async_remote_copy(
            src_ref=chip_tile(p_in), dst_ref=chip_tile(p_in),
            send_sem=fsend.at[s - 1], recv_sem=frecv.at[s - 1],
            device_id={"row": partner}, device_id_type=MESH,
        ).wait_recv()
    for cp in sends + fwds:
        cp.wait_send()


def gather_rows(w, n_row):
    slots, half, width = w.shape
    steps = n_row // 4
    any_spec = pl.BlockSpec(memory_space=pl.ANY)
    return pl.pallas_call(
        functools.partial(gather_rows_kernel, n_row),
        out_shape=jax.ShapeDtypeStruct((slots, half * n_row, width), w.dtype),
        in_specs=[any_spec],
        out_specs=any_spec,
        scratch_shapes=[
            pltpu.SemaphoreType.DMA(()),
            pltpu.SemaphoreType.DMA(()),
            pltpu.SemaphoreType.DMA(()),
            pltpu.SemaphoreType.DMA((steps,)),
            pltpu.SemaphoreType.DMA((steps,)),
            pltpu.SemaphoreType.DMA((steps - 1,)),
            pltpu.SemaphoreType.DMA((steps - 1,)),
        ],
        compiler_params=pltpu.CompilerParams(collective_id=0, has_side_effects=True),
        cost_estimate=pl.CostEstimate(flops=0, transcendentals=0, bytes_accessed=2 * w.size * n_row),
    )(w)


def scatter_rows_kernel(n_row, x_ref, out_ref, part_buf, send_buf, recv_buf, psend, precv, rsend, rrecv):
    me = lax.axis_index("row")
    n_chip = n_row // 2
    z = me // 2
    c = me % 2
    step_dir = 1 - 2 * c
    partner = z * 2 + (1 - c)
    nxt = ((z + step_dir + n_chip) % n_chip) * 2 + c
    prv = ((z - step_dir + n_chip) % n_chip) * 2 + c
    f32 = jnp.float32

    barrier = pltpu.get_barrier_semaphore()
    for peer in (partner, nxt, prv):
        pl.semaphore_signal(barrier, inc=1, device_id={"row": peer}, device_id_type=MESH)
    pl.semaphore_wait(barrier, 3)

    swap = pltpu.make_async_remote_copy(
        src_ref=x_ref.at[:, :, 1 - c], dst_ref=part_buf, send_sem=psend, recv_sem=precv,
        device_id={"row": partner}, device_id_type=MESH,
    )
    swap.start()
    swap.wait_recv()

    def chip_part(q):
        return x_ref[:, q, c].astype(f32) + part_buf[:, q].astype(f32)

    sends = []
    for s in range(1, n_chip):
        q = (z - s * step_dir + n_chip * n_chip) % n_chip
        if s == 1:
            send_buf[s - 1] = chip_part(q)
        else:
            send_buf[s - 1] = recv_buf[s - 2] + chip_part(q)
        ring = pltpu.make_async_remote_copy(
            src_ref=send_buf.at[s - 1], dst_ref=recv_buf.at[s - 1],
            send_sem=rsend.at[s - 1], recv_sem=rrecv.at[s - 1],
            device_id={"row": nxt}, device_id_type=MESH,
        )
        ring.start()
        sends.append(ring)
        ring.wait_recv()
    out_ref[...] = (recv_buf[n_chip - 2] + chip_part(z)).astype(out_ref.dtype)
    swap.wait_send()
    for cp in sends:
        cp.wait_send()


def scatter_rows(x, n_row):
    slots, height, width = x.shape
    n_chip = n_row // 2
    half = height // n_row
    x5 = x.reshape(slots, n_chip, 2, half, width)
    vmem = pl.BlockSpec(memory_space=pltpu.VMEM)
    return pl.pallas_call(
        functools.partial(scatter_rows_kernel, n_row),
        out_shape=jax.ShapeDtypeStruct((slots, half, width), x.dtype),
        in_specs=[vmem],
        out_specs=vmem,
        scratch_shapes=[
            pltpu.VMEM((slots, n_chip, half, width), x.dtype),
            pltpu.VMEM((n_chip - 1, slots, half, width), jnp.float32),
            pltpu.VMEM((n_chip - 1, slots, half, width), jnp.float32),
            pltpu.SemaphoreType.DMA(()),
            pltpu.SemaphoreType.DMA(()),
            pltpu.SemaphoreType.DMA((n_chip - 1,)),
            pltpu.SemaphoreType.DMA((n_chip - 1,)),
        ],
        compiler_params=pltpu.CompilerParams(
            collective_id=1, has_side_effects=True, vmem_limit_bytes=48 * 1024 * 1024
        ),
        cost_estimate=pl.CostEstimate(
            flops=x.size, transcendentals=0, bytes_accessed=4 * x.size
        ),
    )(x5)


def core_kernel(
    slots, gr_ref, ur_ref, dc_ref, p_hbm, w_hbm, panel_hbm, tiles_hbm,
    p_buf, w_buf, out_acc, in_acc, gath, tstage, pstage, isem, tsem, psem,
):
    f32 = jnp.float32
    bf16 = jnp.bfloat16
    peers, _, rows, chunk = p_buf.shape
    per = chunk // BS
    tn = (((0,), (0,)), ((), ()))
    nt = (((1,), (1,)), ((), ()))
    cp_w = pltpu.make_async_copy(w_hbm, w_buf, isem.at[0])
    cp_w.start()
    cp_p = pltpu.make_async_copy(p_hbm, p_buf, isem.at[1])
    cp_p.start()
    out_acc[...] = jnp.zeros_like(out_acc)
    in_acc[...] = jnp.zeros_like(in_acc)
    cp_w.wait()
    cp_p.wait()

    def col(b):
        return pl.ds(pl.multiple_of(b * BS, BS), BS)

    def block(which, b):
        return p_buf[b // per, which, :, pl.ds(pl.multiple_of((b % per) * BS, BS), BS)]

    def body(f, carry):
        for k in range(KG):
            ks = pl.ds(k * BS, BS)
            gath[0, :, ks] = block(0, gr_ref[f, k])
            gath[1, :, ks] = block(0, ur_ref[f, k])
            gath[2, :, ks] = block(1, dc_ref[f, k])
        gw = w_buf[f]
        uw = w_buf[slots + f]
        dw = w_buf[2 * slots + f]
        gate = jnp.dot(gath[0], gw, preferred_element_type=f32)
        up = jnp.dot(gath[1], uw, preferred_element_type=f32)
        hg = jnp.dot(gath[2], dw, preferred_element_type=f32)
        sg = 1.0 / (1.0 + jnp.exp(-gate))
        silu = gate * sg
        hidden = (silu * up).astype(bf16)
        gg = (hg * up * sg * (1.0 + gate * (1.0 - sg))).astype(bf16)
        ug = (hg * silu).astype(bf16)
        po = lax.dot_general(hidden, dw, nt, preferred_element_type=f32)
        pg = lax.dot_general(gg, gw, nt, preferred_element_type=f32)
        pu = lax.dot_general(ug, uw, nt, preferred_element_type=f32)
        for k in range(KG):
            ks = slice(k * BS, (k + 1) * BS)
            out_acc[:, col(dc_ref[f, k])] += po[:, ks]
            in_acc[:, col(gr_ref[f, k])] += pg[:, ks]
            in_acc[:, col(ur_ref[f, k])] += pu[:, ks]
        tstage[f] = lax.dot_general(gath[0], gg, tn, preferred_element_type=f32).astype(bf16)
        tstage[slots + f] = lax.dot_general(gath[1], ug, tn, preferred_element_type=f32).astype(bf16)
        tstage[2 * slots + f] = lax.dot_general(gath[2], hidden, tn, preferred_element_type=f32).astype(bf16)
        for part in range(3):
            s = part * slots + f
            pltpu.make_async_copy(tstage.at[s], tiles_hbm.at[s], tsem.at[s]).start()
        return carry

    lax.fori_loop(0, slots, body, 0)
    outs = []
    for j in range(peers):
        cs = pl.ds(j * chunk, chunk)
        pstage[j, 0] = out_acc[:, cs].astype(bf16)
        pstage[j, 1] = in_acc[:, cs].astype(bf16)
        cp = pltpu.make_async_copy(pstage.at[j], panel_hbm.at[j], psem.at[j])
        cp.start()
        outs.append(cp)
    for s in range(3 * slots):
        pltpu.make_async_copy(tstage.at[s], tiles_hbm.at[s], tsem.at[s]).wait()
    for cp in outs:
        cp.wait()


def core(panels, tiles, gate_rows, up_rows, down_columns):
    slots = gate_rows.shape[0]
    peers, _, rows, chunk = panels.shape
    width = peers * chunk
    smem = pl.BlockSpec(memory_space=pltpu.SMEM)
    any_spec = pl.BlockSpec(memory_space=pl.ANY)
    flops = 2 * rows * BS * BS * slots * KG * 9
    nbytes = 2 * (2 * panels.size + 2 * tiles.size)
    return pl.pallas_call(
        functools.partial(core_kernel, slots),
        out_shape=(
            jax.ShapeDtypeStruct(panels.shape, jnp.bfloat16),
            jax.ShapeDtypeStruct(tiles.shape, jnp.bfloat16),
        ),
        in_specs=[smem, smem, smem, any_spec, any_spec],
        out_specs=(any_spec, any_spec),
        scratch_shapes=[
            pltpu.VMEM(panels.shape, jnp.bfloat16),
            pltpu.VMEM(tiles.shape, jnp.bfloat16),
            pltpu.VMEM((rows, width), jnp.float32),
            pltpu.VMEM((rows, width), jnp.float32),
            pltpu.VMEM((3, rows, KG * BS), jnp.bfloat16),
            pltpu.VMEM(tiles.shape, jnp.bfloat16),
            pltpu.VMEM(panels.shape, jnp.bfloat16),
            pltpu.SemaphoreType.DMA((2,)),
            pltpu.SemaphoreType.DMA((tiles.shape[0],)),
            pltpu.SemaphoreType.DMA((peers,)),
        ],
        compiler_params=pltpu.CompilerParams(vmem_limit_bytes=62 * 1024 * 1024),
        cost_estimate=pl.CostEstimate(
            flops=flops, transcendentals=rows * BS * slots, bytes_accessed=nbytes
        ),
    )(gate_rows, up_rows, down_columns, panels, tiles)


def shards(tokens, out_grad, gate_weight, up_weight, down_weight, gate_rows, up_rows, down_columns):
    owned_slots = gate_weight.shape[0]
    panels = lax.all_gather(jnp.stack([tokens, out_grad]), "col", axis=0)
    n_row = lax.axis_size("row")
    tiles = gather_rows(jnp.concatenate([gate_weight, up_weight, down_weight], axis=0), n_row)
    panel_part, tile_part = core(panels, tiles, gate_rows, up_rows, down_columns)
    tile_sums = scatter_rows(tile_part, n_row)
    peers, _, rows, chunk = panel_part.shape
    panel_sums = lax.psum_scatter(
        panel_part.reshape(peers * 2 * rows, chunk), "col", scatter_dimension=0, tiled=True
    ).reshape(2, rows, chunk)
    return (
        panel_sums[0],
        panel_sums[1],
        tile_sums[:owned_slots],
        tile_sums[owned_slots : 2 * owned_slots],
        tile_sums[2 * owned_slots :],
    )


def solution(mesh):
    in_specs = (
        P("row", "col"),
        P("row", "col"),
        P("col", "row", None),
        P("col", "row", None),
        P("col", "row", None),
        P("col", None),
        P("col", None),
        P("col", None),
    )
    out_specs = (
        P("row", "col"),
        P("row", "col"),
        P("col", "row", None),
        P("col", "row", None),
        P("col", "row", None),
    )
    return jax.shard_map(shards, mesh=mesh, in_specs=in_specs, out_specs=out_specs, check_vma=False)
```

```python
import functools

import jax
import jax.numpy as jnp
from jax import lax
from jax.experimental import pallas as pl
from jax.experimental.pallas import tpu as pltpu
from jax.sharding import PartitionSpec as P

BS = 128
KG = 8
KH = 8


MESH = pl.DeviceIdType.MESH


def gather_rows_kernel(
    n_row, n_col, w_ref, g_ref, out_ref, gout_ref, lsem, psend, precv, rsend, rrecv, fsend, frecv,
    glsem, csend, crecv,
):
    me = lax.axis_index("row")
    mc = lax.axis_index("col")
    n_chip = n_row // 2
    z = me // 2
    c = me % 2
    step_dir = 1 - 2 * c
    partner = z * 2 + (1 - c)
    nxt = ((z + step_dir + n_chip) % n_chip) * 2 + c
    prv = ((z - step_dir + n_chip) % n_chip) * 2 + c
    half = w_ref.shape[1]
    tile = 2 * half

    barrier = pltpu.get_barrier_semaphore()
    for peer in (partner, nxt, prv):
        pl.semaphore_signal(barrier, inc=1, device_id={"row": peer}, device_id_type=MESH)
    for d in range(1, n_col):
        pl.semaphore_signal(
            barrier, inc=1, device_id={"col": (mc + d) % n_col}, device_id_type=MESH
        )
    pl.semaphore_wait(barrier, 3 + n_col - 1)

    glocal = pltpu.make_async_copy(g_ref, gout_ref.at[mc], glsem)
    glocal.start()
    col_sends = []
    for d in range(1, n_col):
        cp = pltpu.make_async_remote_copy(
            src_ref=g_ref, dst_ref=gout_ref.at[mc], send_sem=csend.at[d - 1], recv_sem=crecv.at[d - 1],
            device_id={"col": (mc + d) % n_col}, device_id_type=MESH,
        )
        cp.start()
        col_sends.append(cp)

    def chip_tile(p):
        return out_ref.at[:, pl.ds(pl.multiple_of(p * tile, tile), tile), :]

    own = out_ref.at[:, pl.ds(pl.multiple_of(z * tile + c * half, half), half), :]
    local = pltpu.make_async_copy(w_ref, own, lsem)
    local.start()
    swap = pltpu.make_async_remote_copy(
        src_ref=w_ref, dst_ref=own, send_sem=psend, recv_sem=precv,
        device_id={"row": partner}, device_id_type=MESH,
    )
    swap.start()
    local.wait()
    theirs = out_ref.at[:, pl.ds(pl.multiple_of(z * tile + (1 - c) * half, half), half), :]
    pltpu.make_async_remote_copy(
        src_ref=w_ref, dst_ref=theirs, send_sem=psend, recv_sem=precv,
        device_id={"row": partner}, device_id_type=MESH,
    ).wait_recv()
    swap.wait_send()

    steps = n_chip // 2
    sends = []
    fwds = []
    for s in range(1, steps + 1):
        p_send = (z - (s - 1) * step_dir + n_chip * steps) % n_chip
        p_recv = (z - s * step_dir + n_chip * steps) % n_chip
        ring = pltpu.make_async_remote_copy(
            src_ref=chip_tile(p_send), dst_ref=chip_tile(p_send),
            send_sem=rsend.at[s - 1], recv_sem=rrecv.at[s - 1],
            device_id={"row": nxt}, device_id_type=MESH,
        )
        ring.start()
        sends.append(ring)
        pltpu.make_async_remote_copy(
            src_ref=chip_tile(p_recv), dst_ref=chip_tile(p_recv),
            send_sem=rsend.at[s - 1], recv_sem=rrecv.at[s - 1],
            device_id={"row": prv}, device_id_type=MESH,
        ).wait_recv()
        if s < steps:
            fwd = pltpu.make_async_remote_copy(
                src_ref=chip_tile(p_recv), dst_ref=chip_tile(p_recv),
                send_sem=fsend.at[s - 1], recv_sem=frecv.at[s - 1],
                device_id={"row": partner}, device_id_type=MESH,
            )
            fwd.start()
            fwds.append(fwd)
    for s in range(1, steps):
        p_in = (z + s * step_dir + n_chip * steps) % n_chip
        pltpu.make_async_remote_copy(
            src_ref=chip_tile(p_in), dst_ref=chip_tile(p_in),
            send_sem=fsend.at[s - 1], recv_sem=frecv.at[s - 1],
            device_id={"row": partner}, device_id_type=MESH,
        ).wait_recv()
    for d in range(1, n_col):
        src_col = (mc - d + n_col) % n_col
        pltpu.make_async_remote_copy(
            src_ref=g_ref, dst_ref=gout_ref.at[src_col], send_sem=csend.at[d - 1], recv_sem=crecv.at[d - 1],
            device_id={"col": src_col}, device_id_type=MESH,
        ).wait_recv()
    glocal.wait()
    for cp in sends + fwds + col_sends:
        cp.wait_send()


def gather_rows(w, g, n_row, n_col):
    slots, half, width = w.shape
    steps = n_row // 4
    any_spec = pl.BlockSpec(memory_space=pl.ANY)
    return pl.pallas_call(
        functools.partial(gather_rows_kernel, n_row, n_col),
        out_shape=(
            jax.ShapeDtypeStruct((slots, half * n_row, width), w.dtype),
            jax.ShapeDtypeStruct((n_col,) + g.shape, g.dtype),
        ),
        in_specs=[any_spec, any_spec],
        out_specs=(any_spec, any_spec),
        scratch_shapes=[
            pltpu.SemaphoreType.DMA(()),
            pltpu.SemaphoreType.DMA(()),
            pltpu.SemaphoreType.DMA(()),
            pltpu.SemaphoreType.DMA((steps,)),
            pltpu.SemaphoreType.DMA((steps,)),
            pltpu.SemaphoreType.DMA((steps - 1,)),
            pltpu.SemaphoreType.DMA((steps - 1,)),
            pltpu.SemaphoreType.DMA(()),
            pltpu.SemaphoreType.DMA((n_col - 1,)),
            pltpu.SemaphoreType.DMA((n_col - 1,)),
        ],
        compiler_params=pltpu.CompilerParams(collective_id=0, has_side_effects=True),
        cost_estimate=pl.CostEstimate(
            flops=0, transcendentals=0, bytes_accessed=2 * w.size * n_row + 2 * g.size * n_col
        ),
    )(w, g)


def scatter_rows_kernel(n_row, x_ref, out_ref, part_buf, send_buf, recv_buf, psend, precv, rsend, rrecv):
    me = lax.axis_index("row")
    n_chip = n_row // 2
    z = me // 2
    c = me % 2
    step_dir = 1 - 2 * c
    partner = z * 2 + (1 - c)
    nxt = ((z + step_dir + n_chip) % n_chip) * 2 + c
    prv = ((z - step_dir + n_chip) % n_chip) * 2 + c
    f32 = jnp.float32

    barrier = pltpu.get_barrier_semaphore()
    for peer in (partner, nxt, prv):
        pl.semaphore_signal(barrier, inc=1, device_id={"row": peer}, device_id_type=MESH)
    pl.semaphore_wait(barrier, 3)

    swap = pltpu.make_async_remote_copy(
        src_ref=x_ref.at[:, :, 1 - c], dst_ref=part_buf, send_sem=psend, recv_sem=precv,
        device_id={"row": partner}, device_id_type=MESH,
    )
    swap.start()
    swap.wait_recv()

    def chip_part(q):
        return x_ref[:, q, c].astype(f32) + part_buf[:, q].astype(f32)

    sends = []
    for s in range(1, n_chip):
        q = (z - s * step_dir + n_chip * n_chip) % n_chip
        if s == 1:
            send_buf[s - 1] = chip_part(q)
        else:
            send_buf[s - 1] = recv_buf[s - 2] + chip_part(q)
        ring = pltpu.make_async_remote_copy(
            src_ref=send_buf.at[s - 1], dst_ref=recv_buf.at[s - 1],
            send_sem=rsend.at[s - 1], recv_sem=rrecv.at[s - 1],
            device_id={"row": nxt}, device_id_type=MESH,
        )
        ring.start()
        sends.append(ring)
        ring.wait_recv()
    out_ref[...] = (recv_buf[n_chip - 2] + chip_part(z)).astype(out_ref.dtype)
    swap.wait_send()
    for cp in sends:
        cp.wait_send()


def scatter_rows(x, n_row):
    slots, height, width = x.shape
    n_chip = n_row // 2
    half = height // n_row
    x5 = x.reshape(slots, n_chip, 2, half, width)
    vmem = pl.BlockSpec(memory_space=pltpu.VMEM)
    return pl.pallas_call(
        functools.partial(scatter_rows_kernel, n_row),
        out_shape=jax.ShapeDtypeStruct((slots, half, width), x.dtype),
        in_specs=[vmem],
        out_specs=vmem,
        scratch_shapes=[
            pltpu.VMEM((slots, n_chip, half, width), x.dtype),
            pltpu.VMEM((n_chip - 1, slots, half, width), jnp.float32),
            pltpu.VMEM((n_chip - 1, slots, half, width), jnp.float32),
            pltpu.SemaphoreType.DMA(()),
            pltpu.SemaphoreType.DMA(()),
            pltpu.SemaphoreType.DMA((n_chip - 1,)),
            pltpu.SemaphoreType.DMA((n_chip - 1,)),
        ],
        compiler_params=pltpu.CompilerParams(
            collective_id=1, has_side_effects=True, vmem_limit_bytes=48 * 1024 * 1024
        ),
        cost_estimate=pl.CostEstimate(
            flops=x.size, transcendentals=0, bytes_accessed=4 * x.size
        ),
    )(x5)


def core_kernel(
    slots, gr_ref, ur_ref, dc_ref, x_hbm, g_hbm, w_hbm, panel_hbm, tiles_hbm,
    p_buf, w_buf, out_acc, in_acc, gath, tstage, pstage, isem, tsem, psem,
):
    f32 = jnp.float32
    bf16 = jnp.bfloat16
    peers, _, rows, chunk = p_buf.shape
    per = chunk // BS
    tn = (((0,), (0,)), ((), ()))
    nt = (((1,), (1,)), ((), ()))
    cp_w = pltpu.make_async_copy(w_hbm, w_buf, isem.at[0])
    cp_w.start()
    cp_x = pltpu.make_async_copy(x_hbm, p_buf.at[:, 0], isem.at[1])
    cp_x.start()
    cp_g = pltpu.make_async_copy(g_hbm, p_buf.at[:, 1], isem.at[2])
    cp_g.start()
    out_acc[...] = jnp.zeros_like(out_acc)
    in_acc[...] = jnp.zeros_like(in_acc)
    cp_w.wait()
    cp_x.wait()
    cp_g.wait()

    def col(b):
        return pl.ds(pl.multiple_of(b * BS, BS), BS)

    def block(which, b):
        return p_buf[b // per, which, :, pl.ds(pl.multiple_of((b % per) * BS, BS), BS)]

    def body(f, carry):
        for k in range(KG):
            ks = pl.ds(k * BS, BS)
            gath[0, :, ks] = block(0, gr_ref[f, k])
            gath[1, :, ks] = block(0, ur_ref[f, k])
            gath[2, :, ks] = block(1, dc_ref[f, k])
        gw = w_buf[f]
        uw = w_buf[slots + f]
        dw = w_buf[2 * slots + f]
        gate = jnp.dot(gath[0], gw, preferred_element_type=f32)
        up = jnp.dot(gath[1], uw, preferred_element_type=f32)
        hg = jnp.dot(gath[2], dw, preferred_element_type=f32)
        sg = 1.0 / (1.0 + jnp.exp(-gate))
        silu = gate * sg
        hidden = (silu * up).astype(bf16)
        gg = (hg * up * sg * (1.0 + gate * (1.0 - sg))).astype(bf16)
        ug = (hg * silu).astype(bf16)
        po = lax.dot_general(hidden, dw, nt, preferred_element_type=f32)
        pg = lax.dot_general(gg, gw, nt, preferred_element_type=f32)
        pu = lax.dot_general(ug, uw, nt, preferred_element_type=f32)
        for k in range(KG):
            ks = slice(k * BS, (k + 1) * BS)
            out_acc[:, col(dc_ref[f, k])] += po[:, ks]
            in_acc[:, col(gr_ref[f, k])] += pg[:, ks]
            in_acc[:, col(ur_ref[f, k])] += pu[:, ks]
        tstage[f] = lax.dot_general(gath[0], gg, tn, preferred_element_type=f32).astype(bf16)
        tstage[slots + f] = lax.dot_general(gath[1], ug, tn, preferred_element_type=f32).astype(bf16)
        tstage[2 * slots + f] = lax.dot_general(gath[2], hidden, tn, preferred_element_type=f32).astype(bf16)
        for part in range(3):
            s = part * slots + f
            pltpu.make_async_copy(tstage.at[s], tiles_hbm.at[s], tsem.at[s]).start()
        return carry

    lax.fori_loop(0, slots, body, 0)
    outs = []
    for j in range(peers):
        cs = pl.ds(j * chunk, chunk)
        pstage[j, 0] = out_acc[:, cs].astype(bf16)
        pstage[j, 1] = in_acc[:, cs].astype(bf16)
        cp = pltpu.make_async_copy(pstage.at[j], panel_hbm.at[j], psem.at[j])
        cp.start()
        outs.append(cp)
    for s in range(3 * slots):
        pltpu.make_async_copy(tstage.at[s], tiles_hbm.at[s], tsem.at[s]).wait()
    for cp in outs:
        cp.wait()


def core(x_panel, g_panel, tiles, gate_rows, up_rows, down_columns):
    slots = gate_rows.shape[0]
    peers, rows, chunk = x_panel.shape
    panels = jax.ShapeDtypeStruct((peers, 2, rows, chunk), x_panel.dtype)
    width = peers * chunk
    smem = pl.BlockSpec(memory_space=pltpu.SMEM)
    any_spec = pl.BlockSpec(memory_space=pl.ANY)
    flops = 2 * rows * BS * BS * slots * KG * 9
    nbytes = 2 * (4 * x_panel.size + 2 * tiles.size)
    return pl.pallas_call(
        functools.partial(core_kernel, slots),
        out_shape=(
            jax.ShapeDtypeStruct(panels.shape, jnp.bfloat16),
            jax.ShapeDtypeStruct(tiles.shape, jnp.bfloat16),
        ),
        in_specs=[smem, smem, smem, any_spec, any_spec, any_spec],
        out_specs=(any_spec, any_spec),
        scratch_shapes=[
            pltpu.VMEM(panels.shape, jnp.bfloat16),
            pltpu.VMEM(tiles.shape, jnp.bfloat16),
            pltpu.VMEM((rows, width), jnp.float32),
            pltpu.VMEM((rows, width), jnp.float32),
            pltpu.VMEM((3, rows, KG * BS), jnp.bfloat16),
            pltpu.VMEM(tiles.shape, jnp.bfloat16),
            pltpu.VMEM(panels.shape, jnp.bfloat16),
            pltpu.SemaphoreType.DMA((3,)),
            pltpu.SemaphoreType.DMA((tiles.shape[0],)),
            pltpu.SemaphoreType.DMA((peers,)),
        ],
        compiler_params=pltpu.CompilerParams(vmem_limit_bytes=62 * 1024 * 1024),
        cost_estimate=pl.CostEstimate(
            flops=flops, transcendentals=rows * BS * slots, bytes_accessed=nbytes
        ),
    )(gate_rows, up_rows, down_columns, x_panel, g_panel, tiles)


def shards(tokens, out_grad, gate_weight, up_weight, down_weight, gate_rows, up_rows, down_columns):
    owned_slots = gate_weight.shape[0]
    x_panel = lax.all_gather(tokens, "col", axis=0)
    n_row = lax.axis_size("row")
    n_col = lax.axis_size("col")
    tiles, g_panel = gather_rows(
        jnp.concatenate([gate_weight, up_weight, down_weight], axis=0), out_grad, n_row, n_col
    )
    panel_part, tile_part = core(x_panel, g_panel, tiles, gate_rows, up_rows, down_columns)
    tile_sums = scatter_rows(tile_part, n_row)
    peers, _, rows, chunk = panel_part.shape
    panel_sums = lax.psum_scatter(
        panel_part.reshape(peers * 2 * rows, chunk), "col", scatter_dimension=0, tiled=True
    ).reshape(2, rows, chunk)
    return (
        panel_sums[0],
        panel_sums[1],
        tile_sums[:owned_slots],
        tile_sums[owned_slots : 2 * owned_slots],
        tile_sums[2 * owned_slots :],
    )


def solution(mesh):
    in_specs = (
        P("row", "col"),
        P("row", "col"),
        P("col", "row", None),
        P("col", "row", None),
        P("col", "row", None),
        P("col", None),
        P("col", None),
        P("col", None),
    )
    out_specs = (
        P("row", "col"),
        P("row", "col"),
        P("col", "row", None),
        P("col", "row", None),
        P("col", "row", None),
    )
    return jax.shard_map(shards, mesh=mesh, in_specs=in_specs, out_specs=out_specs, check_vma=False)
```

```python
import functools

import jax
import jax.numpy as jnp
from jax import lax
from jax.experimental import pallas as pl
from jax.experimental.pallas import tpu as pltpu
from jax.sharding import PartitionSpec as P

BS = 128
KG = 8
KH = 8


MESH = pl.DeviceIdType.MESH


def gather_rows_kernel(n_row, w_ref, out_ref, lsem, psend, precv, rsend, rrecv, fsend, frecv):
    me = lax.axis_index("row")
    n_chip = n_row // 2
    z = me // 2
    c = me % 2
    step_dir = 1 - 2 * c
    partner = z * 2 + (1 - c)
    nxt = ((z + step_dir + n_chip) % n_chip) * 2 + c
    prv = ((z - step_dir + n_chip) % n_chip) * 2 + c
    half = w_ref.shape[1]
    tile = 2 * half

    barrier = pltpu.get_barrier_semaphore()
    for peer in (partner, nxt, prv):
        pl.semaphore_signal(barrier, inc=1, device_id={"row": peer}, device_id_type=MESH)
    pl.semaphore_wait(barrier, 3)

    def chip_tile(p):
        return out_ref.at[:, pl.ds(pl.multiple_of(p * tile, tile), tile), :]

    own = out_ref.at[:, pl.ds(pl.multiple_of(z * tile + c * half, half), half), :]
    local = pltpu.make_async_copy(w_ref, own, lsem)
    local.start()
    swap = pltpu.make_async_remote_copy(
        src_ref=w_ref, dst_ref=own, send_sem=psend, recv_sem=precv,
        device_id={"row": partner}, device_id_type=MESH,
    )
    swap.start()
    local.wait()
    theirs = out_ref.at[:, pl.ds(pl.multiple_of(z * tile + (1 - c) * half, half), half), :]
    pltpu.make_async_remote_copy(
        src_ref=w_ref, dst_ref=theirs, send_sem=psend, recv_sem=precv,
        device_id={"row": partner}, device_id_type=MESH,
    ).wait_recv()
    swap.wait_send()

    steps = n_chip // 2
    sends = []
    fwds = []
    for s in range(1, steps + 1):
        p_send = (z - (s - 1) * step_dir + n_chip * steps) % n_chip
        p_recv = (z - s * step_dir + n_chip * steps) % n_chip
        ring = pltpu.make_async_remote_copy(
            src_ref=chip_tile(p_send), dst_ref=chip_tile(p_send),
            send_sem=rsend.at[s - 1], recv_sem=rrecv.at[s - 1],
            device_id={"row": nxt}, device_id_type=MESH,
        )
        ring.start()
        sends.append(ring)
        pltpu.make_async_remote_copy(
            src_ref=chip_tile(p_recv), dst_ref=chip_tile(p_recv),
            send_sem=rsend.at[s - 1], recv_sem=rrecv.at[s - 1],
            device_id={"row": prv}, device_id_type=MESH,
        ).wait_recv()
        if s < steps:
            fwd = pltpu.make_async_remote_copy(
                src_ref=chip_tile(p_recv), dst_ref=chip_tile(p_recv),
                send_sem=fsend.at[s - 1], recv_sem=frecv.at[s - 1],
                device_id={"row": partner}, device_id_type=MESH,
            )
            fwd.start()
            fwds.append(fwd)
    for s in range(1, steps):
        p_in = (z + s * step_dir + n_chip * steps) % n_chip
        pltpu.make_async_remote_copy(
            src_ref=chip_tile(p_in), dst_ref=chip_tile(p_in),
            send_sem=fsend.at[s - 1], recv_sem=frecv.at[s - 1],
            device_id={"row": partner}, device_id_type=MESH,
        ).wait_recv()
    for cp in sends + fwds:
        cp.wait_send()


def gather_rows(w, n_row):
    slots, half, width = w.shape
    steps = n_row // 4
    any_spec = pl.BlockSpec(memory_space=pl.ANY)
    return pl.pallas_call(
        functools.partial(gather_rows_kernel, n_row),
        out_shape=jax.ShapeDtypeStruct((slots, half * n_row, width), w.dtype),
        in_specs=[any_spec],
        out_specs=any_spec,
        scratch_shapes=[
            pltpu.SemaphoreType.DMA(()),
            pltpu.SemaphoreType.DMA(()),
            pltpu.SemaphoreType.DMA(()),
            pltpu.SemaphoreType.DMA((steps,)),
            pltpu.SemaphoreType.DMA((steps,)),
            pltpu.SemaphoreType.DMA((steps - 1,)),
            pltpu.SemaphoreType.DMA((steps - 1,)),
        ],
        compiler_params=pltpu.CompilerParams(collective_id=0, has_side_effects=True),
        cost_estimate=pl.CostEstimate(flops=0, transcendentals=0, bytes_accessed=2 * w.size * n_row),
    )(w)


def scatter_rows_kernel(n_row, x_ref, out_ref, part_buf, send_buf, recv_buf, psend, precv, rsend, rrecv):
    me = lax.axis_index("row")
    n_chip = n_row // 2
    z = me // 2
    c = me % 2
    step_dir = 1 - 2 * c
    partner = z * 2 + (1 - c)
    nxt = ((z + step_dir + n_chip) % n_chip) * 2 + c
    prv = ((z - step_dir + n_chip) % n_chip) * 2 + c
    f32 = jnp.float32

    barrier = pltpu.get_barrier_semaphore()
    for peer in (partner, nxt, prv):
        pl.semaphore_signal(barrier, inc=1, device_id={"row": peer}, device_id_type=MESH)
    pl.semaphore_wait(barrier, 3)

    swap = pltpu.make_async_remote_copy(
        src_ref=x_ref.at[:, :, 1 - c], dst_ref=part_buf, send_sem=psend, recv_sem=precv,
        device_id={"row": partner}, device_id_type=MESH,
    )
    swap.start()
    swap.wait_recv()

    def chip_part(q):
        return x_ref[:, q, c].astype(f32) + part_buf[:, q].astype(f32)

    sends = []
    for s in range(1, n_chip):
        q = (z - s * step_dir + n_chip * n_chip) % n_chip
        if s == 1:
            send_buf[s - 1] = chip_part(q)
        else:
            send_buf[s - 1] = recv_buf[s - 2] + chip_part(q)
        ring = pltpu.make_async_remote_copy(
            src_ref=send_buf.at[s - 1], dst_ref=recv_buf.at[s - 1],
            send_sem=rsend.at[s - 1], recv_sem=rrecv.at[s - 1],
            device_id={"row": nxt}, device_id_type=MESH,
        )
        ring.start()
        sends.append(ring)
        ring.wait_recv()
    out_ref[...] = (recv_buf[n_chip - 2] + chip_part(z)).astype(out_ref.dtype)
    swap.wait_send()
    for cp in sends:
        cp.wait_send()


def scatter_rows(x, n_row):
    slots, height, width = x.shape
    n_chip = n_row // 2
    half = height // n_row
    x5 = x.reshape(slots, n_chip, 2, half, width)
    vmem = pl.BlockSpec(memory_space=pltpu.VMEM)
    return pl.pallas_call(
        functools.partial(scatter_rows_kernel, n_row),
        out_shape=jax.ShapeDtypeStruct((slots, half, width), x.dtype),
        in_specs=[vmem],
        out_specs=vmem,
        scratch_shapes=[
            pltpu.VMEM((slots, n_chip, half, width), x.dtype),
            pltpu.VMEM((n_chip - 1, slots, half, width), jnp.float32),
            pltpu.VMEM((n_chip - 1, slots, half, width), jnp.float32),
            pltpu.SemaphoreType.DMA(()),
            pltpu.SemaphoreType.DMA(()),
            pltpu.SemaphoreType.DMA((n_chip - 1,)),
            pltpu.SemaphoreType.DMA((n_chip - 1,)),
        ],
        compiler_params=pltpu.CompilerParams(
            collective_id=1, has_side_effects=True, vmem_limit_bytes=48 * 1024 * 1024
        ),
        cost_estimate=pl.CostEstimate(
            flops=x.size, transcendentals=0, bytes_accessed=4 * x.size
        ),
    )(x5)


def core_kernel(
    slots, gr_ref, ur_ref, dc_ref, p_hbm, w_hbm, panel_hbm, tiles_hbm,
    p_buf, w_buf, out_acc, in_acc, gath, tstage, pstage, isem, tsem, psem,
):
    f32 = jnp.float32
    bf16 = jnp.bfloat16
    peers, _, rows, chunk = p_buf.shape
    per = chunk // BS
    tn = (((0,), (0,)), ((), ()))
    nt = (((1,), (1,)), ((), ()))
    cp_w = pltpu.make_async_copy(w_hbm, w_buf, isem.at[0])
    cp_w.start()
    cp_p = pltpu.make_async_copy(p_hbm, p_buf, isem.at[1])
    cp_p.start()
    out_acc[...] = jnp.zeros_like(out_acc)
    in_acc[...] = jnp.zeros_like(in_acc)
    cp_w.wait()
    cp_p.wait()

    def col(b):
        return pl.ds(pl.multiple_of(b * BS, BS), BS)

    def block(which, b):
        return p_buf[b // per, which, :, pl.ds(pl.multiple_of((b % per) * BS, BS), BS)]

    def body(f, carry):
        gbuf = gath.at[f % 2]
        for k in range(KG):
            ks = pl.ds(k * BS, BS)
            gbuf[0, :, ks] = block(0, gr_ref[f, k])
            gbuf[1, :, ks] = block(0, ur_ref[f, k])
            gbuf[2, :, ks] = block(1, dc_ref[f, k])
        gw = w_buf[f]
        uw = w_buf[slots + f]
        dw = w_buf[2 * slots + f]
        gate = jnp.dot(gbuf[0], gw, preferred_element_type=f32)
        up = jnp.dot(gbuf[1], uw, preferred_element_type=f32)
        hg = jnp.dot(gbuf[2], dw, preferred_element_type=f32)
        sg = 1.0 / (1.0 + jnp.exp(-gate))
        silu = gate * sg
        hidden = (silu * up).astype(bf16)
        gg = (hg * up * sg * (1.0 + gate * (1.0 - sg))).astype(bf16)
        ug = (hg * silu).astype(bf16)
        po = lax.dot_general(hidden, dw, nt, preferred_element_type=f32)
        pg = lax.dot_general(gg, gw, nt, preferred_element_type=f32)
        pu = lax.dot_general(ug, uw, nt, preferred_element_type=f32)
        for k in range(KG):
            ks = slice(k * BS, (k + 1) * BS)
            out_acc[:, col(dc_ref[f, k])] += po[:, ks]
            in_acc[:, col(gr_ref[f, k])] += pg[:, ks]
            in_acc[:, col(ur_ref[f, k])] += pu[:, ks]
        tstage[f] = lax.dot_general(gbuf[0], gg, tn, preferred_element_type=f32).astype(bf16)
        tstage[slots + f] = lax.dot_general(gbuf[1], ug, tn, preferred_element_type=f32).astype(bf16)
        tstage[2 * slots + f] = lax.dot_general(gbuf[2], hidden, tn, preferred_element_type=f32).astype(bf16)
        for part in range(3):
            s = part * slots + f
            pltpu.make_async_copy(tstage.at[s], tiles_hbm.at[s], tsem.at[s]).start()
        return carry

    lax.fori_loop(0, slots, body, 0, unroll=True)
    outs = []
    for j in range(peers):
        cs = pl.ds(j * chunk, chunk)
        pstage[j, 0] = out_acc[:, cs].astype(bf16)
        pstage[j, 1] = in_acc[:, cs].astype(bf16)
        cp = pltpu.make_async_copy(pstage.at[j], panel_hbm.at[j], psem.at[j])
        cp.start()
        outs.append(cp)
    for s in range(3 * slots):
        pltpu.make_async_copy(tstage.at[s], tiles_hbm.at[s], tsem.at[s]).wait()
    for cp in outs:
        cp.wait()


def core(panels, tiles, gate_rows, up_rows, down_columns):
    slots = gate_rows.shape[0]
    peers, _, rows, chunk = panels.shape
    width = peers * chunk
    smem = pl.BlockSpec(memory_space=pltpu.SMEM)
    any_spec = pl.BlockSpec(memory_space=pl.ANY)
    flops = 2 * rows * BS * BS * slots * KG * 9
    nbytes = 2 * (2 * panels.size + 2 * tiles.size)
    return pl.pallas_call(
        functools.partial(core_kernel, slots),
        out_shape=(
            jax.ShapeDtypeStruct(panels.shape, jnp.bfloat16),
            jax.ShapeDtypeStruct(tiles.shape, jnp.bfloat16),
        ),
        in_specs=[smem, smem, smem, any_spec, any_spec],
        out_specs=(any_spec, any_spec),
        scratch_shapes=[
            pltpu.VMEM(panels.shape, jnp.bfloat16),
            pltpu.VMEM(tiles.shape, jnp.bfloat16),
            pltpu.VMEM((rows, width), jnp.float32),
            pltpu.VMEM((rows, width), jnp.float32),
            pltpu.VMEM((2, 3, rows, KG * BS), jnp.bfloat16),
            pltpu.VMEM(tiles.shape, jnp.bfloat16),
            pltpu.VMEM(panels.shape, jnp.bfloat16),
            pltpu.SemaphoreType.DMA((2,)),
            pltpu.SemaphoreType.DMA((tiles.shape[0],)),
            pltpu.SemaphoreType.DMA((peers,)),
        ],
        compiler_params=pltpu.CompilerParams(vmem_limit_bytes=62 * 1024 * 1024),
        cost_estimate=pl.CostEstimate(
            flops=flops, transcendentals=rows * BS * slots, bytes_accessed=nbytes
        ),
    )(gate_rows, up_rows, down_columns, panels, tiles)


def shards(tokens, out_grad, gate_weight, up_weight, down_weight, gate_rows, up_rows, down_columns):
    owned_slots = gate_weight.shape[0]
    panels = lax.all_gather(jnp.stack([tokens, out_grad]), "col", axis=0)
    n_row = lax.axis_size("row")
    tiles = gather_rows(jnp.concatenate([gate_weight, up_weight, down_weight], axis=0), n_row)
    panel_part, tile_part = core(panels, tiles, gate_rows, up_rows, down_columns)
    tile_sums = scatter_rows(tile_part, n_row)
    peers, _, rows, chunk = panel_part.shape
    panel_sums = lax.psum_scatter(
        panel_part.reshape(peers * 2 * rows, chunk), "col", scatter_dimension=0, tiled=True
    ).reshape(2, rows, chunk)
    return (
        panel_sums[0],
        panel_sums[1],
        tile_sums[:owned_slots],
        tile_sums[owned_slots : 2 * owned_slots],
        tile_sums[2 * owned_slots :],
    )


def solution(mesh):
    in_specs = (
        P("row", "col"),
        P("row", "col"),
        P("col", "row", None),
        P("col", "row", None),
        P("col", "row", None),
        P("col", None),
        P("col", None),
        P("col", None),
    )
    out_specs = (
        P("row", "col"),
        P("row", "col"),
        P("col", "row", None),
        P("col", "row", None),
        P("col", "row", None),
    )
    return jax.shard_map(shards, mesh=mesh, in_specs=in_specs, out_specs=out_specs, check_vma=False)
```

```python
import functools

import jax
import jax.numpy as jnp
from jax import lax
from jax.experimental import pallas as pl
from jax.experimental.pallas import tpu as pltpu
from jax.sharding import PartitionSpec as P

BS = 128
KG = 8
KH = 8


MESH = pl.DeviceIdType.MESH


def gather_rows_kernel(n_row, w_ref, out_ref, lsem, psend, precv, rsend, rrecv, fsend, frecv):
    me = lax.axis_index("row")
    n_chip = n_row // 2
    z = me // 2
    c = me % 2
    step_dir = 1 - 2 * c
    partner = z * 2 + (1 - c)
    nxt = ((z + step_dir + n_chip) % n_chip) * 2 + c
    prv = ((z - step_dir + n_chip) % n_chip) * 2 + c
    half = w_ref.shape[1]
    tile = 2 * half

    barrier = pltpu.get_barrier_semaphore()
    for peer in (partner, nxt, prv):
        pl.semaphore_signal(barrier, inc=1, device_id={"row": peer}, device_id_type=MESH)
    pl.semaphore_wait(barrier, 3)

    def chip_tile(p):
        return out_ref.at[:, pl.ds(pl.multiple_of(p * tile, tile), tile), :]

    own = out_ref.at[:, pl.ds(pl.multiple_of(z * tile + c * half, half), half), :]
    local = pltpu.make_async_copy(w_ref, own, lsem)
    local.start()
    swap = pltpu.make_async_remote_copy(
        src_ref=w_ref, dst_ref=own, send_sem=psend, recv_sem=precv,
        device_id={"row": partner}, device_id_type=MESH,
    )
    swap.start()
    local.wait()
    theirs = out_ref.at[:, pl.ds(pl.multiple_of(z * tile + (1 - c) * half, half), half), :]
    pltpu.make_async_remote_copy(
        src_ref=w_ref, dst_ref=theirs, send_sem=psend, recv_sem=precv,
        device_id={"row": partner}, device_id_type=MESH,
    ).wait_recv()
    swap.wait_send()

    steps = n_chip // 2
    sends = []
    fwds = []
    for s in range(1, steps + 1):
        p_send = (z - (s - 1) * step_dir + n_chip * steps) % n_chip
        p_recv = (z - s * step_dir + n_chip * steps) % n_chip
        ring = pltpu.make_async_remote_copy(
            src_ref=chip_tile(p_send), dst_ref=chip_tile(p_send),
            send_sem=rsend.at[s - 1], recv_sem=rrecv.at[s - 1],
            device_id={"row": nxt}, device_id_type=MESH,
        )
        ring.start()
        sends.append(ring)
        pltpu.make_async_remote_copy(
            src_ref=chip_tile(p_recv), dst_ref=chip_tile(p_recv),
            send_sem=rsend.at[s - 1], recv_sem=rrecv.at[s - 1],
            device_id={"row": prv}, device_id_type=MESH,
        ).wait_recv()
        if s < steps:
            fwd = pltpu.make_async_remote_copy(
                src_ref=chip_tile(p_recv), dst_ref=chip_tile(p_recv),
                send_sem=fsend.at[s - 1], recv_sem=frecv.at[s - 1],
                device_id={"row": partner}, device_id_type=MESH,
            )
            fwd.start()
            fwds.append(fwd)
    for s in range(1, steps):
        p_in = (z + s * step_dir + n_chip * steps) % n_chip
        pltpu.make_async_remote_copy(
            src_ref=chip_tile(p_in), dst_ref=chip_tile(p_in),
            send_sem=fsend.at[s - 1], recv_sem=frecv.at[s - 1],
            device_id={"row": partner}, device_id_type=MESH,
        ).wait_recv()
    for cp in sends + fwds:
        cp.wait_send()


def gather_rows(w, n_row):
    slots, half, width = w.shape
    steps = n_row // 4
    any_spec = pl.BlockSpec(memory_space=pl.ANY)
    return pl.pallas_call(
        functools.partial(gather_rows_kernel, n_row),
        out_shape=jax.ShapeDtypeStruct((slots, half * n_row, width), w.dtype),
        in_specs=[any_spec],
        out_specs=any_spec,
        scratch_shapes=[
            pltpu.SemaphoreType.DMA(()),
            pltpu.SemaphoreType.DMA(()),
            pltpu.SemaphoreType.DMA(()),
            pltpu.SemaphoreType.DMA((steps,)),
            pltpu.SemaphoreType.DMA((steps,)),
            pltpu.SemaphoreType.DMA((steps - 1,)),
            pltpu.SemaphoreType.DMA((steps - 1,)),
        ],
        compiler_params=pltpu.CompilerParams(collective_id=0, has_side_effects=True),
        cost_estimate=pl.CostEstimate(flops=0, transcendentals=0, bytes_accessed=2 * w.size * n_row),
    )(w)


def scatter_rows_kernel(n_row, x_ref, out_ref, part_buf, send_buf, recv_buf, psend, precv, rsend, rrecv):
    me = lax.axis_index("row")
    n_chip = n_row // 2
    z = me // 2
    c = me % 2
    step_dir = 1 - 2 * c
    partner = z * 2 + (1 - c)
    nxt = ((z + step_dir + n_chip) % n_chip) * 2 + c
    prv = ((z - step_dir + n_chip) % n_chip) * 2 + c
    f32 = jnp.float32

    barrier = pltpu.get_barrier_semaphore()
    for peer in (partner, nxt, prv):
        pl.semaphore_signal(barrier, inc=1, device_id={"row": peer}, device_id_type=MESH)
    pl.semaphore_wait(barrier, 3)

    swap = pltpu.make_async_remote_copy(
        src_ref=x_ref.at[:, :, 1 - c], dst_ref=part_buf, send_sem=psend, recv_sem=precv,
        device_id={"row": partner}, device_id_type=MESH,
    )
    swap.start()
    swap.wait_recv()

    def chip_part(q):
        return x_ref[:, q, c].astype(f32) + part_buf[:, q].astype(f32)

    sends = []
    for s in range(1, n_chip):
        q = (z - s * step_dir + n_chip * n_chip) % n_chip
        if s == 1:
            send_buf[s - 1] = chip_part(q)
        else:
            send_buf[s - 1] = recv_buf[s - 2] + chip_part(q)
        ring = pltpu.make_async_remote_copy(
            src_ref=send_buf.at[s - 1], dst_ref=recv_buf.at[s - 1],
            send_sem=rsend.at[s - 1], recv_sem=rrecv.at[s - 1],
            device_id={"row": nxt}, device_id_type=MESH,
        )
        ring.start()
        sends.append(ring)
        ring.wait_recv()
    out_ref[...] = (recv_buf[n_chip - 2] + chip_part(z)).astype(out_ref.dtype)
    swap.wait_send()
    for cp in sends:
        cp.wait_send()


def scatter_rows(x, n_row):
    slots, height, width = x.shape
    n_chip = n_row // 2
    half = height // n_row
    x5 = x.reshape(slots, n_chip, 2, half, width)
    vmem = pl.BlockSpec(memory_space=pltpu.VMEM)
    return pl.pallas_call(
        functools.partial(scatter_rows_kernel, n_row),
        out_shape=jax.ShapeDtypeStruct((slots, half, width), x.dtype),
        in_specs=[vmem],
        out_specs=vmem,
        scratch_shapes=[
            pltpu.VMEM((slots, n_chip, half, width), x.dtype),
            pltpu.VMEM((n_chip - 1, slots, half, width), jnp.float32),
            pltpu.VMEM((n_chip - 1, slots, half, width), jnp.float32),
            pltpu.SemaphoreType.DMA(()),
            pltpu.SemaphoreType.DMA(()),
            pltpu.SemaphoreType.DMA((n_chip - 1,)),
            pltpu.SemaphoreType.DMA((n_chip - 1,)),
        ],
        compiler_params=pltpu.CompilerParams(
            collective_id=1, has_side_effects=True, vmem_limit_bytes=48 * 1024 * 1024
        ),
        cost_estimate=pl.CostEstimate(
            flops=x.size, transcendentals=0, bytes_accessed=4 * x.size
        ),
    )(x5)


def core_kernel(
    slots, gr_ref, ur_ref, dc_ref, p_hbm, w_hbm, panel_hbm, acts_ref,
    p_buf, w_buf, out_acc, in_acc, gath, pstage, isem, psem,
):
    f32 = jnp.float32
    bf16 = jnp.bfloat16
    peers, _, rows, chunk = p_buf.shape
    per = chunk // BS
    nt = (((1,), (1,)), ((), ()))
    cp_w = pltpu.make_async_copy(w_hbm, w_buf, isem.at[0])
    cp_w.start()
    cp_p = pltpu.make_async_copy(p_hbm, p_buf, isem.at[1])
    cp_p.start()
    out_acc[...] = jnp.zeros_like(out_acc)
    in_acc[...] = jnp.zeros_like(in_acc)
    cp_w.wait()
    cp_p.wait()

    def col(b):
        return pl.ds(pl.multiple_of(b * BS, BS), BS)

    def block(which, b):
        return p_buf[b // per, which, :, pl.ds(pl.multiple_of((b % per) * BS, BS), BS)]

    def body(f, carry):
        for k in range(KG):
            ks = pl.ds(k * BS, BS)
            gath[0, :, ks] = block(0, gr_ref[f, k])
            gath[1, :, ks] = block(0, ur_ref[f, k])
            gath[2, :, ks] = block(1, dc_ref[f, k])
        gw = w_buf[f]
        uw = w_buf[slots + f]
        dw = w_buf[2 * slots + f]
        gate = jnp.dot(gath[0], gw, preferred_element_type=f32)
        up = jnp.dot(gath[1], uw, preferred_element_type=f32)
        hg = jnp.dot(gath[2], dw, preferred_element_type=f32)
        sg = 1.0 / (1.0 + jnp.exp(-gate))
        silu = gate * sg
        hidden = (silu * up).astype(bf16)
        gg = (hg * up * sg * (1.0 + gate * (1.0 - sg))).astype(bf16)
        ug = (hg * silu).astype(bf16)
        acts_ref[0, f] = hidden
        acts_ref[1, f] = gg
        acts_ref[2, f] = ug
        po = lax.dot_general(hidden, dw, nt, preferred_element_type=f32)
        pg = lax.dot_general(gg, gw, nt, preferred_element_type=f32)
        pu = lax.dot_general(ug, uw, nt, preferred_element_type=f32)
        for k in range(KG):
            ks = slice(k * BS, (k + 1) * BS)
            out_acc[:, col(dc_ref[f, k])] += po[:, ks]
            in_acc[:, col(gr_ref[f, k])] += pg[:, ks]
            in_acc[:, col(ur_ref[f, k])] += pu[:, ks]
        return carry

    lax.fori_loop(0, slots, body, 0)
    outs = []
    for j in range(peers):
        cs = pl.ds(j * chunk, chunk)
        pstage[j, 0] = out_acc[:, cs].astype(bf16)
        pstage[j, 1] = in_acc[:, cs].astype(bf16)
        cp = pltpu.make_async_copy(pstage.at[j], panel_hbm.at[j], psem.at[j])
        cp.start()
        outs.append(cp)
    for cp in outs:
        cp.wait()


def tile_kernel(slots, gr_ref, ur_ref, dc_ref, p_hbm, acts_ref, tiles_hbm, p_buf, gath, tstage, isem, tsem):
    f32 = jnp.float32
    bf16 = jnp.bfloat16
    peers, _, rows, chunk = p_buf.shape
    per = chunk // BS
    tn = (((0,), (0,)), ((), ()))
    cp_p = pltpu.make_async_copy(p_hbm, p_buf, isem)
    cp_p.start()
    cp_p.wait()

    def block(which, b):
        return p_buf[b // per, which, :, pl.ds(pl.multiple_of((b % per) * BS, BS), BS)]

    def body(f, carry):
        for k in range(KG):
            ks = pl.ds(k * BS, BS)
            gath[0, :, ks] = block(0, gr_ref[f, k])
            gath[1, :, ks] = block(0, ur_ref[f, k])
            gath[2, :, ks] = block(1, dc_ref[f, k])
        tstage[f] = lax.dot_general(gath[0], acts_ref[1, f], tn, preferred_element_type=f32).astype(bf16)
        tstage[slots + f] = lax.dot_general(gath[1], acts_ref[2, f], tn, preferred_element_type=f32).astype(bf16)
        tstage[2 * slots + f] = lax.dot_general(gath[2], acts_ref[0, f], tn, preferred_element_type=f32).astype(bf16)
        for part in range(3):
            s = part * slots + f
            pltpu.make_async_copy(tstage.at[s], tiles_hbm.at[s], tsem.at[s]).start()
        return carry

    lax.fori_loop(0, slots, body, 0)
    for s in range(3 * slots):
        pltpu.make_async_copy(tstage.at[s], tiles_hbm.at[s], tsem.at[s]).wait()


def core(panels, tiles, gate_rows, up_rows, down_columns):
    slots = gate_rows.shape[0]
    peers, _, rows, chunk = panels.shape
    width = peers * chunk
    smem = pl.BlockSpec(memory_space=pltpu.SMEM)
    vmem = pl.BlockSpec(memory_space=pltpu.VMEM)
    any_spec = pl.BlockSpec(memory_space=pl.ANY)
    dot_flops = 2 * rows * BS * BS * slots * KG
    panel_part, acts = pl.pallas_call(
        functools.partial(core_kernel, slots),
        out_shape=(
            jax.ShapeDtypeStruct(panels.shape, jnp.bfloat16),
            jax.ShapeDtypeStruct((3, slots, rows, BS), jnp.bfloat16),
        ),
        in_specs=[smem, smem, smem, any_spec, any_spec],
        out_specs=(any_spec, vmem),
        scratch_shapes=[
            pltpu.VMEM(panels.shape, jnp.bfloat16),
            pltpu.VMEM(tiles.shape, jnp.bfloat16),
            pltpu.VMEM((rows, width), jnp.float32),
            pltpu.VMEM((rows, width), jnp.float32),
            pltpu.VMEM((3, rows, KG * BS), jnp.bfloat16),
            pltpu.VMEM(panels.shape, jnp.bfloat16),
            pltpu.SemaphoreType.DMA((2,)),
            pltpu.SemaphoreType.DMA((peers,)),
        ],
        compiler_params=pltpu.CompilerParams(vmem_limit_bytes=62 * 1024 * 1024),
        cost_estimate=pl.CostEstimate(
            flops=6 * dot_flops, transcendentals=rows * BS * slots,
            bytes_accessed=2 * (2 * panels.size + tiles.size),
        ),
    )(gate_rows, up_rows, down_columns, panels, tiles)
    tile_part = pl.pallas_call(
        functools.partial(tile_kernel, slots),
        out_shape=jax.ShapeDtypeStruct(tiles.shape, jnp.bfloat16),
        in_specs=[smem, smem, smem, any_spec, vmem],
        out_specs=any_spec,
        scratch_shapes=[
            pltpu.VMEM(panels.shape, jnp.bfloat16),
            pltpu.VMEM((3, rows, KG * BS), jnp.bfloat16),
            pltpu.VMEM(tiles.shape, jnp.bfloat16),
            pltpu.SemaphoreType.DMA(()),
            pltpu.SemaphoreType.DMA((tiles.shape[0],)),
        ],
        compiler_params=pltpu.CompilerParams(vmem_limit_bytes=40 * 1024 * 1024),
        cost_estimate=pl.CostEstimate(
            flops=3 * dot_flops, transcendentals=0,
            bytes_accessed=2 * (panels.size + tiles.size),
        ),
    )(gate_rows, up_rows, down_columns, panels, acts)
    return panel_part, tile_part


def shards(tokens, out_grad, gate_weight, up_weight, down_weight, gate_rows, up_rows, down_columns):
    owned_slots = gate_weight.shape[0]
    panels = lax.all_gather(jnp.stack([tokens, out_grad]), "col", axis=0)
    n_row = lax.axis_size("row")
    tiles = gather_rows(jnp.concatenate([gate_weight, up_weight, down_weight], axis=0), n_row)
    panel_part, tile_part = core(panels, tiles, gate_rows, up_rows, down_columns)
    tile_sums = scatter_rows(tile_part, n_row)
    peers, _, rows, chunk = panel_part.shape
    panel_sums = lax.psum_scatter(
        panel_part.reshape(peers * 2 * rows, chunk), "col", scatter_dimension=0, tiled=True
    ).reshape(2, rows, chunk)
    return (
        panel_sums[0],
        panel_sums[1],
        tile_sums[:owned_slots],
        tile_sums[owned_slots : 2 * owned_slots],
        tile_sums[2 * owned_slots :],
    )


def solution(mesh):
    in_specs = (
        P("row", "col"),
        P("row", "col"),
        P("col", "row", None),
        P("col", "row", None),
        P("col", "row", None),
        P("col", None),
        P("col", None),
        P("col", None),
    )
    out_specs = (
        P("row", "col"),
        P("row", "col"),
        P("col", "row", None),
        P("col", "row", None),
        P("col", "row", None),
    )
    return jax.shard_map(shards, mesh=mesh, in_specs=in_specs, out_specs=out_specs, check_vma=False)
```

```python
import functools

import jax
import jax.numpy as jnp
from jax import lax
from jax.experimental import pallas as pl
from jax.experimental.pallas import tpu as pltpu
from jax.sharding import PartitionSpec as P

BS = 128
KG = 8
KH = 8


MESH = pl.DeviceIdType.MESH


def gather_rows_kernel(n_row, w_ref, out_ref, lsem, psend, precv, rsend, rrecv, fsend, frecv):
    me = lax.axis_index("row")
    n_chip = n_row // 2
    z = me // 2
    c = me % 2
    step_dir = 1 - 2 * c
    partner = z * 2 + (1 - c)
    nxt = ((z + step_dir + n_chip) % n_chip) * 2 + c
    prv = ((z - step_dir + n_chip) % n_chip) * 2 + c
    half = w_ref.shape[1]
    tile = 2 * half

    barrier = pltpu.get_barrier_semaphore()
    for peer in (partner, nxt, prv):
        pl.semaphore_signal(barrier, inc=1, device_id={"row": peer}, device_id_type=MESH)
    pl.semaphore_wait(barrier, 3)

    def chip_tile(p):
        return out_ref.at[:, pl.ds(pl.multiple_of(p * tile, tile), tile), :]

    own = out_ref.at[:, pl.ds(pl.multiple_of(z * tile + c * half, half), half), :]
    local = pltpu.make_async_copy(w_ref, own, lsem)
    local.start()
    swap = pltpu.make_async_remote_copy(
        src_ref=w_ref, dst_ref=own, send_sem=psend, recv_sem=precv,
        device_id={"row": partner}, device_id_type=MESH,
    )
    swap.start()
    local.wait()
    theirs = out_ref.at[:, pl.ds(pl.multiple_of(z * tile + (1 - c) * half, half), half), :]
    pltpu.make_async_remote_copy(
        src_ref=w_ref, dst_ref=theirs, send_sem=psend, recv_sem=precv,
        device_id={"row": partner}, device_id_type=MESH,
    ).wait_recv()
    swap.wait_send()

    steps = n_chip // 2
    sends = []
    fwds = []
    for s in range(1, steps + 1):
        p_send = (z - (s - 1) * step_dir + n_chip * steps) % n_chip
        p_recv = (z - s * step_dir + n_chip * steps) % n_chip
        ring = pltpu.make_async_remote_copy(
            src_ref=chip_tile(p_send), dst_ref=chip_tile(p_send),
            send_sem=rsend.at[s - 1], recv_sem=rrecv.at[s - 1],
            device_id={"row": nxt}, device_id_type=MESH,
        )
        ring.start()
        sends.append(ring)
        pltpu.make_async_remote_copy(
            src_ref=chip_tile(p_recv), dst_ref=chip_tile(p_recv),
            send_sem=rsend.at[s - 1], recv_sem=rrecv.at[s - 1],
            device_id={"row": prv}, device_id_type=MESH,
        ).wait_recv()
        if s < steps:
            fwd = pltpu.make_async_remote_copy(
                src_ref=chip_tile(p_recv), dst_ref=chip_tile(p_recv),
                send_sem=fsend.at[s - 1], recv_sem=frecv.at[s - 1],
                device_id={"row": partner}, device_id_type=MESH,
            )
            fwd.start()
            fwds.append(fwd)
    for s in range(1, steps):
        p_in = (z + s * step_dir + n_chip * steps) % n_chip
        pltpu.make_async_remote_copy(
            src_ref=chip_tile(p_in), dst_ref=chip_tile(p_in),
            send_sem=fsend.at[s - 1], recv_sem=frecv.at[s - 1],
            device_id={"row": partner}, device_id_type=MESH,
        ).wait_recv()
    for cp in sends + fwds:
        cp.wait_send()


def gather_rows(w, n_row):
    slots, half, width = w.shape
    steps = n_row // 4
    any_spec = pl.BlockSpec(memory_space=pl.ANY)
    return pl.pallas_call(
        functools.partial(gather_rows_kernel, n_row),
        out_shape=jax.ShapeDtypeStruct((slots, half * n_row, width), w.dtype),
        in_specs=[any_spec],
        out_specs=any_spec,
        scratch_shapes=[
            pltpu.SemaphoreType.DMA(()),
            pltpu.SemaphoreType.DMA(()),
            pltpu.SemaphoreType.DMA(()),
            pltpu.SemaphoreType.DMA((steps,)),
            pltpu.SemaphoreType.DMA((steps,)),
            pltpu.SemaphoreType.DMA((steps - 1,)),
            pltpu.SemaphoreType.DMA((steps - 1,)),
        ],
        compiler_params=pltpu.CompilerParams(collective_id=0, has_side_effects=True),
        cost_estimate=pl.CostEstimate(flops=0, transcendentals=0, bytes_accessed=2 * w.size * n_row),
    )(w)


def scatter_rows_kernel(n_row, x_ref, out_ref, part_buf, send_buf, recv_buf, psend, precv, rsend, rrecv):
    me = lax.axis_index("row")
    n_chip = n_row // 2
    z = me // 2
    c = me % 2
    step_dir = 1 - 2 * c
    partner = z * 2 + (1 - c)
    nxt = ((z + step_dir + n_chip) % n_chip) * 2 + c
    prv = ((z - step_dir + n_chip) % n_chip) * 2 + c
    f32 = jnp.float32

    barrier = pltpu.get_barrier_semaphore()
    for peer in (partner, nxt, prv):
        pl.semaphore_signal(barrier, inc=1, device_id={"row": peer}, device_id_type=MESH)
    pl.semaphore_wait(barrier, 3)

    swap = pltpu.make_async_remote_copy(
        src_ref=x_ref.at[:, :, 1 - c], dst_ref=part_buf, send_sem=psend, recv_sem=precv,
        device_id={"row": partner}, device_id_type=MESH,
    )
    swap.start()
    swap.wait_recv()

    def chip_part(q):
        return x_ref[:, q, c].astype(f32) + part_buf[:, q].astype(f32)

    sends = []
    for s in range(1, n_chip):
        q = (z - s * step_dir + n_chip * n_chip) % n_chip
        if s == 1:
            send_buf[s - 1] = chip_part(q)
        else:
            send_buf[s - 1] = recv_buf[s - 2] + chip_part(q)
        ring = pltpu.make_async_remote_copy(
            src_ref=send_buf.at[s - 1], dst_ref=recv_buf.at[s - 1],
            send_sem=rsend.at[s - 1], recv_sem=rrecv.at[s - 1],
            device_id={"row": nxt}, device_id_type=MESH,
        )
        ring.start()
        sends.append(ring)
        ring.wait_recv()
    out_ref[...] = (recv_buf[n_chip - 2] + chip_part(z)).astype(out_ref.dtype)
    swap.wait_send()
    for cp in sends:
        cp.wait_send()


def scatter_rows(x, n_row):
    slots, height, width = x.shape
    n_chip = n_row // 2
    half = height // n_row
    x5 = x.reshape(slots, n_chip, 2, half, width)
    vmem = pl.BlockSpec(memory_space=pltpu.VMEM)
    return pl.pallas_call(
        functools.partial(scatter_rows_kernel, n_row),
        out_shape=jax.ShapeDtypeStruct((slots, half, width), x.dtype),
        in_specs=[vmem],
        out_specs=vmem,
        scratch_shapes=[
            pltpu.VMEM((slots, n_chip, half, width), x.dtype),
            pltpu.VMEM((n_chip - 1, slots, half, width), jnp.float32),
            pltpu.VMEM((n_chip - 1, slots, half, width), jnp.float32),
            pltpu.SemaphoreType.DMA(()),
            pltpu.SemaphoreType.DMA(()),
            pltpu.SemaphoreType.DMA((n_chip - 1,)),
            pltpu.SemaphoreType.DMA((n_chip - 1,)),
        ],
        compiler_params=pltpu.CompilerParams(
            collective_id=1, has_side_effects=True, vmem_limit_bytes=48 * 1024 * 1024
        ),
        cost_estimate=pl.CostEstimate(
            flops=x.size, transcendentals=0, bytes_accessed=4 * x.size
        ),
    )(x5)


def core_kernel(
    slots, gr_ref, ur_ref, dc_ref, p_hbm, w_hbm, panel_hbm, acts_ref,
    p_buf, w_buf, out_acc, in_acc, gath, pstage, isem, psem, wsem,
):
    f32 = jnp.float32
    bf16 = jnp.bfloat16
    peers, _, rows, chunk = p_buf.shape
    per = chunk // BS
    nt = (((1,), (1,)), ((), ()))
    def wcopy(s):
        return pltpu.make_async_copy(w_hbm.at[s], w_buf.at[s], wsem.at[s])

    for part in range(3):
        wcopy(part * slots).start()
    cp_p = pltpu.make_async_copy(p_hbm, p_buf, isem.at[1])
    cp_p.start()
    for f in range(1, slots):
        for part in range(3):
            wcopy(part * slots + f).start()
    out_acc[...] = jnp.zeros_like(out_acc)
    in_acc[...] = jnp.zeros_like(in_acc)
    cp_p.wait()

    def col(b):
        return pl.ds(pl.multiple_of(b * BS, BS), BS)

    def block(which, b):
        return p_buf[b // per, which, :, pl.ds(pl.multiple_of((b % per) * BS, BS), BS)]

    def body(f, carry):
        for k in range(KG):
            ks = pl.ds(k * BS, BS)
            gath[0, :, ks] = block(0, gr_ref[f, k])
            gath[1, :, ks] = block(0, ur_ref[f, k])
            gath[2, :, ks] = block(1, dc_ref[f, k])
        for part in range(3):
            wcopy(part * slots + f).wait()
        gw = w_buf[f]
        uw = w_buf[slots + f]
        dw = w_buf[2 * slots + f]
        gate = jnp.dot(gath[0], gw, preferred_element_type=f32)
        up = jnp.dot(gath[1], uw, preferred_element_type=f32)
        hg = jnp.dot(gath[2], dw, preferred_element_type=f32)
        sg = 1.0 / (1.0 + jnp.exp(-gate))
        silu = gate * sg
        hidden = (silu * up).astype(bf16)
        gg = (hg * up * sg * (1.0 + gate * (1.0 - sg))).astype(bf16)
        ug = (hg * silu).astype(bf16)
        acts_ref[0, f] = hidden
        acts_ref[1, f] = gg
        acts_ref[2, f] = ug
        po = lax.dot_general(hidden, dw, nt, preferred_element_type=f32)
        pg = lax.dot_general(gg, gw, nt, preferred_element_type=f32)
        pu = lax.dot_general(ug, uw, nt, preferred_element_type=f32)
        for k in range(KG):
            ks = slice(k * BS, (k + 1) * BS)
            out_acc[:, col(dc_ref[f, k])] += po[:, ks]
            in_acc[:, col(gr_ref[f, k])] += pg[:, ks]
            in_acc[:, col(ur_ref[f, k])] += pu[:, ks]
        return carry

    lax.fori_loop(0, slots, body, 0)
    outs = []
    for j in range(peers):
        cs = pl.ds(j * chunk, chunk)
        pstage[j, 0] = out_acc[:, cs].astype(bf16)
        pstage[j, 1] = in_acc[:, cs].astype(bf16)
        cp = pltpu.make_async_copy(pstage.at[j], panel_hbm.at[j], psem.at[j])
        cp.start()
        outs.append(cp)
    for cp in outs:
        cp.wait()


def tile_kernel(slots, gr_ref, ur_ref, dc_ref, p_hbm, acts_ref, tiles_hbm, p_buf, gath, tstage, isem, tsem):
    f32 = jnp.float32
    bf16 = jnp.bfloat16
    peers, _, rows, chunk = p_buf.shape
    per = chunk // BS
    tn = (((0,), (0,)), ((), ()))
    cp_p = pltpu.make_async_copy(p_hbm, p_buf, isem)
    cp_p.start()
    cp_p.wait()

    def block(which, b):
        return p_buf[b // per, which, :, pl.ds(pl.multiple_of((b % per) * BS, BS), BS)]

    def body(f, carry):
        for k in range(KG):
            ks = pl.ds(k * BS, BS)
            gath[0, :, ks] = block(0, gr_ref[f, k])
            gath[1, :, ks] = block(0, ur_ref[f, k])
            gath[2, :, ks] = block(1, dc_ref[f, k])
        tstage[f] = lax.dot_general(gath[0], acts_ref[1, f], tn, preferred_element_type=f32).astype(bf16)
        tstage[slots + f] = lax.dot_general(gath[1], acts_ref[2, f], tn, preferred_element_type=f32).astype(bf16)
        tstage[2 * slots + f] = lax.dot_general(gath[2], acts_ref[0, f], tn, preferred_element_type=f32).astype(bf16)
        for part in range(3):
            s = part * slots + f
            pltpu.make_async_copy(tstage.at[s], tiles_hbm.at[s], tsem.at[s]).start()
        return carry

    lax.fori_loop(0, slots, body, 0)
    for s in range(3 * slots):
        pltpu.make_async_copy(tstage.at[s], tiles_hbm.at[s], tsem.at[s]).wait()


def core(panels, tiles, gate_rows, up_rows, down_columns):
    slots = gate_rows.shape[0]
    peers, _, rows, chunk = panels.shape
    width = peers * chunk
    smem = pl.BlockSpec(memory_space=pltpu.SMEM)
    vmem = pl.BlockSpec(memory_space=pltpu.VMEM)
    any_spec = pl.BlockSpec(memory_space=pl.ANY)
    dot_flops = 2 * rows * BS * BS * slots * KG
    panel_part, acts = pl.pallas_call(
        functools.partial(core_kernel, slots),
        out_shape=(
            jax.ShapeDtypeStruct(panels.shape, jnp.bfloat16),
            jax.ShapeDtypeStruct((3, slots, rows, BS), jnp.bfloat16),
        ),
        in_specs=[smem, smem, smem, any_spec, any_spec],
        out_specs=(any_spec, vmem),
        scratch_shapes=[
            pltpu.VMEM(panels.shape, jnp.bfloat16),
            pltpu.VMEM(tiles.shape, jnp.bfloat16),
            pltpu.VMEM((rows, width), jnp.float32),
            pltpu.VMEM((rows, width), jnp.float32),
            pltpu.VMEM((3, rows, KG * BS), jnp.bfloat16),
            pltpu.VMEM(panels.shape, jnp.bfloat16),
            pltpu.SemaphoreType.DMA((2,)),
            pltpu.SemaphoreType.DMA((peers,)),
            pltpu.SemaphoreType.DMA((tiles.shape[0],)),
        ],
        compiler_params=pltpu.CompilerParams(vmem_limit_bytes=62 * 1024 * 1024),
        cost_estimate=pl.CostEstimate(
            flops=6 * dot_flops, transcendentals=rows * BS * slots,
            bytes_accessed=2 * (2 * panels.size + tiles.size),
        ),
    )(gate_rows, up_rows, down_columns, panels, tiles)
    tile_part = pl.pallas_call(
        functools.partial(tile_kernel, slots),
        out_shape=jax.ShapeDtypeStruct(tiles.shape, jnp.bfloat16),
        in_specs=[smem, smem, smem, any_spec, vmem],
        out_specs=any_spec,
        scratch_shapes=[
            pltpu.VMEM(panels.shape, jnp.bfloat16),
            pltpu.VMEM((3, rows, KG * BS), jnp.bfloat16),
            pltpu.VMEM(tiles.shape, jnp.bfloat16),
            pltpu.SemaphoreType.DMA(()),
            pltpu.SemaphoreType.DMA((tiles.shape[0],)),
        ],
        compiler_params=pltpu.CompilerParams(vmem_limit_bytes=40 * 1024 * 1024),
        cost_estimate=pl.CostEstimate(
            flops=3 * dot_flops, transcendentals=0,
            bytes_accessed=2 * (panels.size + tiles.size),
        ),
    )(gate_rows, up_rows, down_columns, panels, acts)
    return panel_part, tile_part


def shards(tokens, out_grad, gate_weight, up_weight, down_weight, gate_rows, up_rows, down_columns):
    owned_slots = gate_weight.shape[0]
    panels = lax.all_gather(jnp.stack([tokens, out_grad]), "col", axis=0)
    n_row = lax.axis_size("row")
    tiles = gather_rows(jnp.concatenate([gate_weight, up_weight, down_weight], axis=0), n_row)
    panel_part, tile_part = core(panels, tiles, gate_rows, up_rows, down_columns)
    tile_sums = scatter_rows(tile_part, n_row)
    peers, _, rows, chunk = panel_part.shape
    panel_sums = lax.psum_scatter(
        panel_part.reshape(peers * 2 * rows, chunk), "col", scatter_dimension=0, tiled=True
    ).reshape(2, rows, chunk)
    return (
        panel_sums[0],
        panel_sums[1],
        tile_sums[:owned_slots],
        tile_sums[owned_slots : 2 * owned_slots],
        tile_sums[2 * owned_slots :],
    )


def solution(mesh):
    in_specs = (
        P("row", "col"),
        P("row", "col"),
        P("col", "row", None),
        P("col", "row", None),
        P("col", "row", None),
        P("col", None),
        P("col", None),
        P("col", None),
    )
    out_specs = (
        P("row", "col"),
        P("row", "col"),
        P("col", "row", None),
        P("col", "row", None),
        P("col", "row", None),
    )
    return jax.shard_map(shards, mesh=mesh, in_specs=in_specs, out_specs=out_specs, check_vma=False)
```

```python
import functools

import jax
import jax.numpy as jnp
from jax import lax
from jax.experimental import pallas as pl
from jax.experimental.pallas import tpu as pltpu
from jax.sharding import PartitionSpec as P

BS = 128
KG = 8
KH = 8


MESH = pl.DeviceIdType.MESH


def gather_rows_kernel(n_row, w_ref, out_ref, lsem, psend, precv, rsend, rrecv, fsend, frecv):
    me = lax.axis_index("row")
    n_chip = n_row // 2
    z = me // 2
    c = me % 2
    step_dir = 1 - 2 * c
    partner = z * 2 + (1 - c)
    nxt = ((z + step_dir + n_chip) % n_chip) * 2 + c
    prv = ((z - step_dir + n_chip) % n_chip) * 2 + c
    half = w_ref.shape[1]
    tile = 2 * half

    barrier = pltpu.get_barrier_semaphore()
    for peer in (partner, nxt, prv):
        pl.semaphore_signal(barrier, inc=1, device_id={"row": peer}, device_id_type=MESH)
    pl.semaphore_wait(barrier, 3)

    def chip_tile(p):
        return out_ref.at[:, pl.ds(pl.multiple_of(p * tile, tile), tile), :]

    own = out_ref.at[:, pl.ds(pl.multiple_of(z * tile + c * half, half), half), :]
    local = pltpu.make_async_copy(w_ref, own, lsem)
    local.start()
    swap = pltpu.make_async_remote_copy(
        src_ref=w_ref, dst_ref=own, send_sem=psend, recv_sem=precv,
        device_id={"row": partner}, device_id_type=MESH,
    )
    swap.start()
    local.wait()
    theirs = out_ref.at[:, pl.ds(pl.multiple_of(z * tile + (1 - c) * half, half), half), :]
    pltpu.make_async_remote_copy(
        src_ref=w_ref, dst_ref=theirs, send_sem=psend, recv_sem=precv,
        device_id={"row": partner}, device_id_type=MESH,
    ).wait_recv()
    swap.wait_send()

    steps = n_chip // 2
    sends = []
    fwds = []
    for s in range(1, steps + 1):
        p_send = (z - (s - 1) * step_dir + n_chip * steps) % n_chip
        p_recv = (z - s * step_dir + n_chip * steps) % n_chip
        ring = pltpu.make_async_remote_copy(
            src_ref=chip_tile(p_send), dst_ref=chip_tile(p_send),
            send_sem=rsend.at[s - 1], recv_sem=rrecv.at[s - 1],
            device_id={"row": nxt}, device_id_type=MESH,
        )
        ring.start()
        sends.append(ring)
        pltpu.make_async_remote_copy(
            src_ref=chip_tile(p_recv), dst_ref=chip_tile(p_recv),
            send_sem=rsend.at[s - 1], recv_sem=rrecv.at[s - 1],
            device_id={"row": prv}, device_id_type=MESH,
        ).wait_recv()
        if s < steps:
            fwd = pltpu.make_async_remote_copy(
                src_ref=chip_tile(p_recv), dst_ref=chip_tile(p_recv),
                send_sem=fsend.at[s - 1], recv_sem=frecv.at[s - 1],
                device_id={"row": partner}, device_id_type=MESH,
            )
            fwd.start()
            fwds.append(fwd)
    for s in range(1, steps):
        p_in = (z + s * step_dir + n_chip * steps) % n_chip
        pltpu.make_async_remote_copy(
            src_ref=chip_tile(p_in), dst_ref=chip_tile(p_in),
            send_sem=fsend.at[s - 1], recv_sem=frecv.at[s - 1],
            device_id={"row": partner}, device_id_type=MESH,
        ).wait_recv()
    for cp in sends + fwds:
        cp.wait_send()


def gather_rows(w, n_row):
    slots, half, width = w.shape
    steps = n_row // 4
    any_spec = pl.BlockSpec(memory_space=pl.ANY)
    return pl.pallas_call(
        functools.partial(gather_rows_kernel, n_row),
        out_shape=jax.ShapeDtypeStruct((slots, half * n_row, width), w.dtype),
        in_specs=[any_spec],
        out_specs=any_spec,
        scratch_shapes=[
            pltpu.SemaphoreType.DMA(()),
            pltpu.SemaphoreType.DMA(()),
            pltpu.SemaphoreType.DMA(()),
            pltpu.SemaphoreType.DMA((steps,)),
            pltpu.SemaphoreType.DMA((steps,)),
            pltpu.SemaphoreType.DMA((steps - 1,)),
            pltpu.SemaphoreType.DMA((steps - 1,)),
        ],
        compiler_params=pltpu.CompilerParams(collective_id=0, has_side_effects=True),
        cost_estimate=pl.CostEstimate(flops=0, transcendentals=0, bytes_accessed=2 * w.size * n_row),
    )(w)


def scatter_rows_kernel(n_row, x_ref, out_ref, part_buf, send_buf, recv_buf, psend, precv, rsend, rrecv):
    me = lax.axis_index("row")
    n_chip = n_row // 2
    z = me // 2
    c = me % 2
    step_dir = 1 - 2 * c
    partner = z * 2 + (1 - c)
    nxt = ((z + step_dir + n_chip) % n_chip) * 2 + c
    prv = ((z - step_dir + n_chip) % n_chip) * 2 + c
    f32 = jnp.float32

    barrier = pltpu.get_barrier_semaphore()
    for peer in (partner, nxt, prv):
        pl.semaphore_signal(barrier, inc=1, device_id={"row": peer}, device_id_type=MESH)
    pl.semaphore_wait(barrier, 3)

    swap = pltpu.make_async_remote_copy(
        src_ref=x_ref.at[:, :, 1 - c], dst_ref=part_buf, send_sem=psend, recv_sem=precv,
        device_id={"row": partner}, device_id_type=MESH,
    )
    swap.start()
    swap.wait_recv()

    def chip_part(q):
        return x_ref[:, q, c].astype(f32) + part_buf[:, q].astype(f32)

    sends = []
    for s in range(1, n_chip):
        q = (z - s * step_dir + n_chip * n_chip) % n_chip
        if s == 1:
            send_buf[s - 1] = chip_part(q)
        else:
            send_buf[s - 1] = recv_buf[s - 2] + chip_part(q)
        ring = pltpu.make_async_remote_copy(
            src_ref=send_buf.at[s - 1], dst_ref=recv_buf.at[s - 1],
            send_sem=rsend.at[s - 1], recv_sem=rrecv.at[s - 1],
            device_id={"row": nxt}, device_id_type=MESH,
        )
        ring.start()
        sends.append(ring)
        ring.wait_recv()
    out_ref[...] = (recv_buf[n_chip - 2] + chip_part(z)).astype(out_ref.dtype)
    swap.wait_send()
    for cp in sends:
        cp.wait_send()


def scatter_rows(x, n_row):
    slots, height, width = x.shape
    n_chip = n_row // 2
    half = height // n_row
    x5 = x.reshape(slots, n_chip, 2, half, width)
    vmem = pl.BlockSpec(memory_space=pltpu.VMEM)
    return pl.pallas_call(
        functools.partial(scatter_rows_kernel, n_row),
        out_shape=jax.ShapeDtypeStruct((slots, half, width), x.dtype),
        in_specs=[vmem],
        out_specs=vmem,
        scratch_shapes=[
            pltpu.VMEM((slots, n_chip, half, width), x.dtype),
            pltpu.VMEM((n_chip - 1, slots, half, width), jnp.float32),
            pltpu.VMEM((n_chip - 1, slots, half, width), jnp.float32),
            pltpu.SemaphoreType.DMA(()),
            pltpu.SemaphoreType.DMA(()),
            pltpu.SemaphoreType.DMA((n_chip - 1,)),
            pltpu.SemaphoreType.DMA((n_chip - 1,)),
        ],
        compiler_params=pltpu.CompilerParams(
            collective_id=1, has_side_effects=True, vmem_limit_bytes=48 * 1024 * 1024
        ),
        cost_estimate=pl.CostEstimate(
            flops=x.size, transcendentals=0, bytes_accessed=4 * x.size
        ),
    )(x5)


def core_kernel(
    slots, gr_ref, ur_ref, dc_ref, p_hbm, w_hbm, panel_hbm, acts_ref,
    p_buf, w_buf, out_acc, in_acc, gath, pstage, isem, psem, wsem, psem_in,
):
    f32 = jnp.float32
    bf16 = jnp.bfloat16
    peers, _, rows, chunk = p_buf.shape
    per = chunk // BS
    nt = (((1,), (1,)), ((), ()))
    copies = []
    for part in range(3):
        ws = pl.ds(part * slots, slots)
        copies.append(pltpu.make_async_copy(w_hbm.at[ws], w_buf.at[ws], wsem.at[part]))
    for j in range(peers):
        copies.append(pltpu.make_async_copy(p_hbm.at[j], p_buf.at[j], psem_in.at[j]))
    for cp in copies:
        cp.start()
    out_acc[...] = jnp.zeros_like(out_acc)
    in_acc[...] = jnp.zeros_like(in_acc)
    for cp in copies:
        cp.wait()

    def col(b):
        return pl.ds(pl.multiple_of(b * BS, BS), BS)

    def block(which, b):
        return p_buf[b // per, which, :, pl.ds(pl.multiple_of((b % per) * BS, BS), BS)]

    def body(f, carry):
        for k in range(KG):
            ks = pl.ds(k * BS, BS)
            gath[0, :, ks] = block(0, gr_ref[f, k])
            gath[1, :, ks] = block(0, ur_ref[f, k])
            gath[2, :, ks] = block(1, dc_ref[f, k])
        gw = w_buf[f]
        uw = w_buf[slots + f]
        dw = w_buf[2 * slots + f]
        gate = jnp.dot(gath[0], gw, preferred_element_type=f32)
        up = jnp.dot(gath[1], uw, preferred_element_type=f32)
        hg = jnp.dot(gath[2], dw, preferred_element_type=f32)
        sg = 1.0 / (1.0 + jnp.exp(-gate))
        silu = gate * sg
        hidden = (silu * up).astype(bf16)
        gg = (hg * up * sg * (1.0 + gate * (1.0 - sg))).astype(bf16)
        ug = (hg * silu).astype(bf16)
        acts_ref[0, f] = hidden
        acts_ref[1, f] = gg
        acts_ref[2, f] = ug
        po = lax.dot_general(hidden, dw, nt, preferred_element_type=f32)
        pg = lax.dot_general(gg, gw, nt, preferred_element_type=f32)
        pu = lax.dot_general(ug, uw, nt, preferred_element_type=f32)
        for k in range(KG):
            ks = slice(k * BS, (k + 1) * BS)
            out_acc[:, col(dc_ref[f, k])] += po[:, ks]
            in_acc[:, col(gr_ref[f, k])] += pg[:, ks]
            in_acc[:, col(ur_ref[f, k])] += pu[:, ks]
        return carry

    lax.fori_loop(0, slots, body, 0)
    outs = []
    for j in range(peers):
        cs = pl.ds(j * chunk, chunk)
        pstage[j, 0] = out_acc[:, cs].astype(bf16)
        pstage[j, 1] = in_acc[:, cs].astype(bf16)
        cp = pltpu.make_async_copy(pstage.at[j], panel_hbm.at[j], psem.at[j])
        cp.start()
        outs.append(cp)
    for cp in outs:
        cp.wait()


def tile_kernel(slots, gr_ref, ur_ref, dc_ref, p_hbm, acts_ref, tiles_hbm, p_buf, gath, tstage, isem, tsem):
    f32 = jnp.float32
    bf16 = jnp.bfloat16
    peers, _, rows, chunk = p_buf.shape
    per = chunk // BS
    tn = (((0,), (0,)), ((), ()))
    cp_p = pltpu.make_async_copy(p_hbm, p_buf, isem)
    cp_p.start()
    cp_p.wait()

    def block(which, b):
        return p_buf[b // per, which, :, pl.ds(pl.multiple_of((b % per) * BS, BS), BS)]

    def body(f, carry):
        for k in range(KG):
            ks = pl.ds(k * BS, BS)
            gath[0, :, ks] = block(0, gr_ref[f, k])
            gath[1, :, ks] = block(0, ur_ref[f, k])
            gath[2, :, ks] = block(1, dc_ref[f, k])
        tstage[f] = lax.dot_general(gath[0], acts_ref[1, f], tn, preferred_element_type=f32).astype(bf16)
        tstage[slots + f] = lax.dot_general(gath[1], acts_ref[2, f], tn, preferred_element_type=f32).astype(bf16)
        tstage[2 * slots + f] = lax.dot_general(gath[2], acts_ref[0, f], tn, preferred_element_type=f32).astype(bf16)
        for part in range(3):
            s = part * slots + f
            pltpu.make_async_copy(tstage.at[s], tiles_hbm.at[s], tsem.at[s]).start()
        return carry

    lax.fori_loop(0, slots, body, 0)
    for s in range(3 * slots):
        pltpu.make_async_copy(tstage.at[s], tiles_hbm.at[s], tsem.at[s]).wait()


def core(panels, tiles, gate_rows, up_rows, down_columns):
    slots = gate_rows.shape[0]
    peers, _, rows, chunk = panels.shape
    width = peers * chunk
    smem = pl.BlockSpec(memory_space=pltpu.SMEM)
    vmem = pl.BlockSpec(memory_space=pltpu.VMEM)
    any_spec = pl.BlockSpec(memory_space=pl.ANY)
    dot_flops = 2 * rows * BS * BS * slots * KG
    panel_part, acts = pl.pallas_call(
        functools.partial(core_kernel, slots),
        out_shape=(
            jax.ShapeDtypeStruct(panels.shape, jnp.bfloat16),
            jax.ShapeDtypeStruct((3, slots, rows, BS), jnp.bfloat16),
        ),
        in_specs=[smem, smem, smem, any_spec, any_spec],
        out_specs=(any_spec, vmem),
        scratch_shapes=[
            pltpu.VMEM(panels.shape, jnp.bfloat16),
            pltpu.VMEM(tiles.shape, jnp.bfloat16),
            pltpu.VMEM((rows, width), jnp.float32),
            pltpu.VMEM((rows, width), jnp.float32),
            pltpu.VMEM((3, rows, KG * BS), jnp.bfloat16),
            pltpu.VMEM(panels.shape, jnp.bfloat16),
            pltpu.SemaphoreType.DMA((2,)),
            pltpu.SemaphoreType.DMA((peers,)),
            pltpu.SemaphoreType.DMA((3,)),
            pltpu.SemaphoreType.DMA((peers,)),
        ],
        compiler_params=pltpu.CompilerParams(vmem_limit_bytes=62 * 1024 * 1024),
        cost_estimate=pl.CostEstimate(
            flops=6 * dot_flops, transcendentals=rows * BS * slots,
            bytes_accessed=2 * (2 * panels.size + tiles.size),
        ),
    )(gate_rows, up_rows, down_columns, panels, tiles)
    tile_part = pl.pallas_call(
        functools.partial(tile_kernel, slots),
        out_shape=jax.ShapeDtypeStruct(tiles.shape, jnp.bfloat16),
        in_specs=[smem, smem, smem, any_spec, vmem],
        out_specs=any_spec,
        scratch_shapes=[
            pltpu.VMEM(panels.shape, jnp.bfloat16),
            pltpu.VMEM((3, rows, KG * BS), jnp.bfloat16),
            pltpu.VMEM(tiles.shape, jnp.bfloat16),
            pltpu.SemaphoreType.DMA(()),
            pltpu.SemaphoreType.DMA((tiles.shape[0],)),
        ],
        compiler_params=pltpu.CompilerParams(vmem_limit_bytes=40 * 1024 * 1024),
        cost_estimate=pl.CostEstimate(
            flops=3 * dot_flops, transcendentals=0,
            bytes_accessed=2 * (panels.size + tiles.size),
        ),
    )(gate_rows, up_rows, down_columns, panels, acts)
    return panel_part, tile_part


def shards(tokens, out_grad, gate_weight, up_weight, down_weight, gate_rows, up_rows, down_columns):
    owned_slots = gate_weight.shape[0]
    panels = lax.all_gather(jnp.stack([tokens, out_grad]), "col", axis=0)
    n_row = lax.axis_size("row")
    tiles = gather_rows(jnp.concatenate([gate_weight, up_weight, down_weight], axis=0), n_row)
    panel_part, tile_part = core(panels, tiles, gate_rows, up_rows, down_columns)
    tile_sums = scatter_rows(tile_part, n_row)
    peers, _, rows, chunk = panel_part.shape
    panel_sums = lax.psum_scatter(
        panel_part.reshape(peers * 2 * rows, chunk), "col", scatter_dimension=0, tiled=True
    ).reshape(2, rows, chunk)
    return (
        panel_sums[0],
        panel_sums[1],
        tile_sums[:owned_slots],
        tile_sums[owned_slots : 2 * owned_slots],
        tile_sums[2 * owned_slots :],
    )


def solution(mesh):
    in_specs = (
        P("row", "col"),
        P("row", "col"),
        P("col", "row", None),
        P("col", "row", None),
        P("col", "row", None),
        P("col", None),
        P("col", None),
        P("col", None),
    )
    out_specs = (
        P("row", "col"),
        P("row", "col"),
        P("col", "row", None),
        P("col", "row", None),
        P("col", "row", None),
    )
    return jax.shard_map(shards, mesh=mesh, in_specs=in_specs, out_specs=out_specs, check_vma=False)
```

```python
import functools

import jax
import jax.numpy as jnp
from jax import lax
from jax.experimental import pallas as pl
from jax.experimental.pallas import tpu as pltpu
from jax.sharding import PartitionSpec as P

BS = 128
KG = 8
KH = 8


MESH = pl.DeviceIdType.MESH


def gather_rows_kernel(n_row, w_ref, out_ref, lsem, psend, precv, rsend, rrecv, fsend, frecv):
    me = lax.axis_index("row")
    n_chip = n_row // 2
    z = me // 2
    c = me % 2
    step_dir = 1 - 2 * c
    partner = z * 2 + (1 - c)
    nxt = ((z + step_dir + n_chip) % n_chip) * 2 + c
    prv = ((z - step_dir + n_chip) % n_chip) * 2 + c
    half = w_ref.shape[1]
    tile = 2 * half

    barrier = pltpu.get_barrier_semaphore()
    for peer in (partner, nxt, prv):
        pl.semaphore_signal(barrier, inc=1, device_id={"row": peer}, device_id_type=MESH)
    pl.semaphore_wait(barrier, 3)

    def chip_tile(p):
        return out_ref.at[:, pl.ds(pl.multiple_of(p * tile, tile), tile), :]

    own = out_ref.at[:, pl.ds(pl.multiple_of(z * tile + c * half, half), half), :]
    local = pltpu.make_async_copy(w_ref, own, lsem)
    local.start()
    swap = pltpu.make_async_remote_copy(
        src_ref=w_ref, dst_ref=own, send_sem=psend, recv_sem=precv,
        device_id={"row": partner}, device_id_type=MESH,
    )
    swap.start()
    local.wait()
    theirs = out_ref.at[:, pl.ds(pl.multiple_of(z * tile + (1 - c) * half, half), half), :]
    pltpu.make_async_remote_copy(
        src_ref=w_ref, dst_ref=theirs, send_sem=psend, recv_sem=precv,
        device_id={"row": partner}, device_id_type=MESH,
    ).wait_recv()
    swap.wait_send()

    steps = n_chip // 2
    sends = []
    fwds = []
    for s in range(1, steps + 1):
        p_send = (z - (s - 1) * step_dir + n_chip * steps) % n_chip
        p_recv = (z - s * step_dir + n_chip * steps) % n_chip
        ring = pltpu.make_async_remote_copy(
            src_ref=chip_tile(p_send), dst_ref=chip_tile(p_send),
            send_sem=rsend.at[s - 1], recv_sem=rrecv.at[s - 1],
            device_id={"row": nxt}, device_id_type=MESH,
        )
        ring.start()
        sends.append(ring)
        pltpu.make_async_remote_copy(
            src_ref=chip_tile(p_recv), dst_ref=chip_tile(p_recv),
            send_sem=rsend.at[s - 1], recv_sem=rrecv.at[s - 1],
            device_id={"row": prv}, device_id_type=MESH,
        ).wait_recv()
        if s < steps:
            fwd = pltpu.make_async_remote_copy(
                src_ref=chip_tile(p_recv), dst_ref=chip_tile(p_recv),
                send_sem=fsend.at[s - 1], recv_sem=frecv.at[s - 1],
                device_id={"row": partner}, device_id_type=MESH,
            )
            fwd.start()
            fwds.append(fwd)
    for s in range(1, steps):
        p_in = (z + s * step_dir + n_chip * steps) % n_chip
        pltpu.make_async_remote_copy(
            src_ref=chip_tile(p_in), dst_ref=chip_tile(p_in),
            send_sem=fsend.at[s - 1], recv_sem=frecv.at[s - 1],
            device_id={"row": partner}, device_id_type=MESH,
        ).wait_recv()
    for cp in sends + fwds:
        cp.wait_send()


def gather_rows(w, n_row):
    slots, half, width = w.shape
    steps = n_row // 4
    any_spec = pl.BlockSpec(memory_space=pl.ANY)
    return pl.pallas_call(
        functools.partial(gather_rows_kernel, n_row),
        out_shape=jax.ShapeDtypeStruct((slots, half * n_row, width), w.dtype),
        in_specs=[any_spec],
        out_specs=any_spec,
        scratch_shapes=[
            pltpu.SemaphoreType.DMA(()),
            pltpu.SemaphoreType.DMA(()),
            pltpu.SemaphoreType.DMA(()),
            pltpu.SemaphoreType.DMA((steps,)),
            pltpu.SemaphoreType.DMA((steps,)),
            pltpu.SemaphoreType.DMA((steps - 1,)),
            pltpu.SemaphoreType.DMA((steps - 1,)),
        ],
        compiler_params=pltpu.CompilerParams(collective_id=0, has_side_effects=True),
        cost_estimate=pl.CostEstimate(flops=0, transcendentals=0, bytes_accessed=2 * w.size * n_row),
    )(w)


def scatter_rows_kernel(
    n_row, x_ref, out_ref, own_buf, part_buf, send_buf, recv_buf, osem, psend, precv, rsend, rrecv
):
    me = lax.axis_index("row")
    n_chip = n_row // 2
    z = me // 2
    c = me % 2
    step_dir = 1 - 2 * c
    partner = z * 2 + (1 - c)
    nxt = ((z + step_dir + n_chip) % n_chip) * 2 + c
    prv = ((z - step_dir + n_chip) % n_chip) * 2 + c
    f32 = jnp.float32

    own = pltpu.make_async_copy(x_ref.at[:, :, c], own_buf, osem)
    own.start()
    barrier = pltpu.get_barrier_semaphore()
    for peer in (partner, nxt, prv):
        pl.semaphore_signal(barrier, inc=1, device_id={"row": peer}, device_id_type=MESH)
    pl.semaphore_wait(barrier, 3)

    swap = pltpu.make_async_remote_copy(
        src_ref=x_ref.at[:, :, 1 - c], dst_ref=part_buf, send_sem=psend, recv_sem=precv,
        device_id={"row": partner}, device_id_type=MESH,
    )
    swap.start()
    swap.wait_recv()
    own.wait()

    def chip_part(q):
        return own_buf[:, q].astype(f32) + part_buf[:, q].astype(f32)

    sends = []
    for s in range(1, n_chip):
        q = (z - s * step_dir + n_chip * n_chip) % n_chip
        if s == 1:
            send_buf[s - 1] = chip_part(q)
        else:
            send_buf[s - 1] = recv_buf[s - 2] + chip_part(q)
        ring = pltpu.make_async_remote_copy(
            src_ref=send_buf.at[s - 1], dst_ref=recv_buf.at[s - 1],
            send_sem=rsend.at[s - 1], recv_sem=rrecv.at[s - 1],
            device_id={"row": nxt}, device_id_type=MESH,
        )
        ring.start()
        sends.append(ring)
        ring.wait_recv()
    out_ref[...] = (recv_buf[n_chip - 2] + chip_part(z)).astype(out_ref.dtype)
    swap.wait_send()
    for cp in sends:
        cp.wait_send()


def scatter_rows(x, n_row):
    slots, height, width = x.shape
    n_chip = n_row // 2
    half = height // n_row
    x5 = x.reshape(slots, n_chip, 2, half, width)
    vmem = pl.BlockSpec(memory_space=pltpu.VMEM)
    return pl.pallas_call(
        functools.partial(scatter_rows_kernel, n_row),
        out_shape=jax.ShapeDtypeStruct((slots, half, width), x.dtype),
        in_specs=[pl.BlockSpec(memory_space=pl.ANY)],
        out_specs=vmem,
        scratch_shapes=[
            pltpu.VMEM((slots, n_chip, half, width), x.dtype),
            pltpu.VMEM((slots, n_chip, half, width), x.dtype),
            pltpu.VMEM((n_chip - 1, slots, half, width), jnp.float32),
            pltpu.VMEM((n_chip - 1, slots, half, width), jnp.float32),
            pltpu.SemaphoreType.DMA(()),
            pltpu.SemaphoreType.DMA(()),
            pltpu.SemaphoreType.DMA(()),
            pltpu.SemaphoreType.DMA((n_chip - 1,)),
            pltpu.SemaphoreType.DMA((n_chip - 1,)),
        ],
        compiler_params=pltpu.CompilerParams(
            collective_id=1, has_side_effects=True, vmem_limit_bytes=48 * 1024 * 1024
        ),
        cost_estimate=pl.CostEstimate(
            flops=x.size, transcendentals=0, bytes_accessed=4 * x.size
        ),
    )(x5)


def core_kernel(
    slots, gr_ref, ur_ref, dc_ref, p_hbm, w_hbm, panel_hbm, acts_ref,
    p_buf, w_buf, out_acc, in_acc, gath, pstage, isem, psem,
):
    f32 = jnp.float32
    bf16 = jnp.bfloat16
    peers, _, rows, chunk = p_buf.shape
    per = chunk // BS
    nt = (((1,), (1,)), ((), ()))
    cp_w = pltpu.make_async_copy(w_hbm, w_buf, isem.at[0])
    cp_w.start()
    cp_p = pltpu.make_async_copy(p_hbm, p_buf, isem.at[1])
    cp_p.start()
    out_acc[...] = jnp.zeros_like(out_acc)
    in_acc[...] = jnp.zeros_like(in_acc)
    cp_w.wait()
    cp_p.wait()

    def col(b):
        return pl.ds(pl.multiple_of(b * BS, BS), BS)

    def block(which, b):
        return p_buf[b // per, which, :, pl.ds(pl.multiple_of((b % per) * BS, BS), BS)]

    def body(f, carry):
        for k in range(KG):
            ks = pl.ds(k * BS, BS)
            gath[0, :, ks] = block(0, gr_ref[f, k])
            gath[1, :, ks] = block(0, ur_ref[f, k])
            gath[2, :, ks] = block(1, dc_ref[f, k])
        gw = w_buf[f]
        uw = w_buf[slots + f]
        dw = w_buf[2 * slots + f]
        gate = jnp.dot(gath[0], gw, preferred_element_type=f32)
        up = jnp.dot(gath[1], uw, preferred_element_type=f32)
        hg = jnp.dot(gath[2], dw, preferred_element_type=f32)
        sg = 1.0 / (1.0 + jnp.exp(-gate))
        silu = gate * sg
        hidden = (silu * up).astype(bf16)
        gg = (hg * up * sg * (1.0 + gate * (1.0 - sg))).astype(bf16)
        ug = (hg * silu).astype(bf16)
        acts_ref[0, f] = hidden
        acts_ref[1, f] = gg
        acts_ref[2, f] = ug
        po = lax.dot_general(hidden, dw, nt, preferred_element_type=f32)
        pg = lax.dot_general(gg, gw, nt, preferred_element_type=f32)
        pu = lax.dot_general(ug, uw, nt, preferred_element_type=f32)
        for k in range(KG):
            ks = slice(k * BS, (k + 1) * BS)
            out_acc[:, col(dc_ref[f, k])] += po[:, ks]
            in_acc[:, col(gr_ref[f, k])] += pg[:, ks]
            in_acc[:, col(ur_ref[f, k])] += pu[:, ks]
        return carry

    lax.fori_loop(0, slots, body, 0)
    outs = []
    for j in range(peers):
        cs = pl.ds(j * chunk, chunk)
        pstage[j, 0] = out_acc[:, cs].astype(bf16)
        pstage[j, 1] = in_acc[:, cs].astype(bf16)
        cp = pltpu.make_async_copy(pstage.at[j], panel_hbm.at[j], psem.at[j])
        cp.start()
        outs.append(cp)
    for cp in outs:
        cp.wait()


def tile_kernel(slots, gr_ref, ur_ref, dc_ref, p_hbm, acts_ref, tiles_hbm, p_buf, gath, tstage, isem, tsem):
    f32 = jnp.float32
    bf16 = jnp.bfloat16
    peers, _, rows, chunk = p_buf.shape
    per = chunk // BS
    tn = (((0,), (0,)), ((), ()))
    cp_p = pltpu.make_async_copy(p_hbm, p_buf, isem)
    cp_p.start()
    cp_p.wait()

    def block(which, b):
        return p_buf[b // per, which, :, pl.ds(pl.multiple_of((b % per) * BS, BS), BS)]

    def body(f, carry):
        for k in range(KG):
            ks = pl.ds(k * BS, BS)
            gath[0, :, ks] = block(0, gr_ref[f, k])
            gath[1, :, ks] = block(0, ur_ref[f, k])
            gath[2, :, ks] = block(1, dc_ref[f, k])
        tstage[f] = lax.dot_general(gath[0], acts_ref[1, f], tn, preferred_element_type=f32).astype(bf16)
        tstage[slots + f] = lax.dot_general(gath[1], acts_ref[2, f], tn, preferred_element_type=f32).astype(bf16)
        tstage[2 * slots + f] = lax.dot_general(gath[2], acts_ref[0, f], tn, preferred_element_type=f32).astype(bf16)
        for part in range(3):
            s = part * slots + f
            pltpu.make_async_copy(tstage.at[s], tiles_hbm.at[s], tsem.at[s]).start()
        return carry

    lax.fori_loop(0, slots, body, 0)
    for s in range(3 * slots):
        pltpu.make_async_copy(tstage.at[s], tiles_hbm.at[s], tsem.at[s]).wait()


def core(panels, tiles, gate_rows, up_rows, down_columns):
    slots = gate_rows.shape[0]
    peers, _, rows, chunk = panels.shape
    width = peers * chunk
    smem = pl.BlockSpec(memory_space=pltpu.SMEM)
    vmem = pl.BlockSpec(memory_space=pltpu.VMEM)
    any_spec = pl.BlockSpec(memory_space=pl.ANY)
    dot_flops = 2 * rows * BS * BS * slots * KG
    panel_part, acts = pl.pallas_call(
        functools.partial(core_kernel, slots),
        out_shape=(
            jax.ShapeDtypeStruct(panels.shape, jnp.bfloat16),
            jax.ShapeDtypeStruct((3, slots, rows, BS), jnp.bfloat16),
        ),
        in_specs=[smem, smem, smem, any_spec, any_spec],
        out_specs=(any_spec, vmem),
        scratch_shapes=[
            pltpu.VMEM(panels.shape, jnp.bfloat16),
            pltpu.VMEM(tiles.shape, jnp.bfloat16),
            pltpu.VMEM((rows, width), jnp.float32),
            pltpu.VMEM((rows, width), jnp.float32),
            pltpu.VMEM((3, rows, KG * BS), jnp.bfloat16),
            pltpu.VMEM(panels.shape, jnp.bfloat16),
            pltpu.SemaphoreType.DMA((2,)),
            pltpu.SemaphoreType.DMA((peers,)),
        ],
        compiler_params=pltpu.CompilerParams(vmem_limit_bytes=62 * 1024 * 1024),
        cost_estimate=pl.CostEstimate(
            flops=6 * dot_flops, transcendentals=rows * BS * slots,
            bytes_accessed=2 * (2 * panels.size + tiles.size),
        ),
    )(gate_rows, up_rows, down_columns, panels, tiles)
    tile_part = pl.pallas_call(
        functools.partial(tile_kernel, slots),
        out_shape=jax.ShapeDtypeStruct(tiles.shape, jnp.bfloat16),
        in_specs=[smem, smem, smem, any_spec, vmem],
        out_specs=any_spec,
        scratch_shapes=[
            pltpu.VMEM(panels.shape, jnp.bfloat16),
            pltpu.VMEM((3, rows, KG * BS), jnp.bfloat16),
            pltpu.VMEM(tiles.shape, jnp.bfloat16),
            pltpu.SemaphoreType.DMA(()),
            pltpu.SemaphoreType.DMA((tiles.shape[0],)),
        ],
        compiler_params=pltpu.CompilerParams(vmem_limit_bytes=40 * 1024 * 1024),
        cost_estimate=pl.CostEstimate(
            flops=3 * dot_flops, transcendentals=0,
            bytes_accessed=2 * (panels.size + tiles.size),
        ),
    )(gate_rows, up_rows, down_columns, panels, acts)
    return panel_part, tile_part


def shards(tokens, out_grad, gate_weight, up_weight, down_weight, gate_rows, up_rows, down_columns):
    owned_slots = gate_weight.shape[0]
    panels = lax.all_gather(jnp.stack([tokens, out_grad]), "col", axis=0)
    n_row = lax.axis_size("row")
    tiles = gather_rows(jnp.concatenate([gate_weight, up_weight, down_weight], axis=0), n_row)
    panel_part, tile_part = core(panels, tiles, gate_rows, up_rows, down_columns)
    tile_sums = scatter_rows(tile_part, n_row)
    peers, _, rows, chunk = panel_part.shape
    panel_sums = lax.psum_scatter(
        panel_part.reshape(peers * 2 * rows, chunk), "col", scatter_dimension=0, tiled=True
    ).reshape(2, rows, chunk)
    return (
        panel_sums[0],
        panel_sums[1],
        tile_sums[:owned_slots],
        tile_sums[owned_slots : 2 * owned_slots],
        tile_sums[2 * owned_slots :],
    )


def solution(mesh):
    in_specs = (
        P("row", "col"),
        P("row", "col"),
        P("col", "row", None),
        P("col", "row", None),
        P("col", "row", None),
        P("col", None),
        P("col", None),
        P("col", None),
    )
    out_specs = (
        P("row", "col"),
        P("row", "col"),
        P("col", "row", None),
        P("col", "row", None),
        P("col", "row", None),
    )
    return jax.shard_map(shards, mesh=mesh, in_specs=in_specs, out_specs=out_specs, check_vma=False)
```
